32 devices in a mesh: region: 8 (over z, core), state: 4 (over y, x).
Axes of the slice: x: 2, y: 2, z: 4, core: 2. Of those that a mesh axis runs over, the one named last changes fastest.
Arguments:
- state_anom: float32 [8, 16, 256, 512], P('region', 'state'), may hold values from -6 to 6
- obs_anom: float32 [8, 256, 512], P('region', 'state'), may hold values from -6 to 6
- obs_weight: float32 [8, 256, 512], P('region', 'state'), may hold values from -6 to 6
- obs_cell: int32 [8, 256], P('region', 'state'), may hold values from 0 to 255, as said below
- sector_of: int32 [8], replicated, may hold values from 0 to 7, as said below
Outputs:
- increment: float32 [8, 16, 256, 512], P('region', 'state')
The draws below stay inside these ranges and needn't reach their ends.
Inputs may be any that keep to these rules, and one draw needn't show every extreme that they name: `obs_cell`: each entry is lon * 8 + lat with lon in 0..31 and lat in 0..7. Within each aligned block of 64 entries along the observation dimension the entries do not decrease; in each such block between 8 and 16 entries have lon < 8, and between 8 and 16 have lon >= 24; the bound 16 is reached on both sides in every draw. `sector_of`: A permutation: every region holds a different sector.
All inputs are finite; a program needn't handle non-finite values.
Results may differ from the reference program's by a relative error of at most 0.0003.
Values sent between devices are 32-bit elements; how exact they have to be, the bound alone decides.
No kernel may reach another device: no remote copies, remote signals or barrier semaphores. Data moves between devices by JAX's collectives and lax.ppermute only.
A program may use at most 64 MiB of HBM per device.

```python
import jax
import jax.numpy as jnp
from jax import lax

MEMBERS = 512
SECT_W = 32
LAT = 8
HALF = 4
OBS_DEV = 64
CAP = 16
COLS = 256
REGIONS = 8
LEVELS = 16
OBS_REG = 256
N_REGION = 8
N_STATE = 4


def draw_obs_cell(key, part):
    devices = REGIONS * N_STATE
    keys = jax.random.split(key, 6)
    left_count = jax.random.randint(keys[0], (devices,), CAP // 2, CAP + 1).at[0].set(CAP)
    right_count = jax.random.randint(keys[1], (devices,), CAP // 2, CAP + 1).at[devices - 1].set(CAP)
    slots = jnp.arange(OBS_DEV, dtype=jnp.int32)[None, :]
    edge_band = 2 * HALF
    lon_left = jax.random.randint(keys[2], (devices, OBS_DEV), 0, edge_band)
    lon_middle = jax.random.randint(keys[3], (devices, OBS_DEV), edge_band, SECT_W - edge_band)
    lon_right = jax.random.randint(keys[4], (devices, OBS_DEV), SECT_W - edge_band, SECT_W)
    lon_off = jnp.where(slots < left_count[:, None], lon_left, jnp.where(slots >= OBS_DEV - right_count[:, None], lon_right, lon_middle))
    lat_cell = jax.random.randint(keys[5], (devices, OBS_DEV), 0, LAT)
    cells = jnp.sort(lon_off * LAT + lat_cell, axis=1)
    return cells.reshape(REGIONS, OBS_REG).astype(jnp.int32)


def draw_sector_of(key, part):
    middle = REGIONS // 2
    region_ids = jnp.arange(REGIONS, dtype=jnp.int32)
    sectors = jax.random.permutation(jax.random.fold_in(key, 7), REGIONS).astype(jnp.int32)
    target = (sectors[0] + 1) % REGIONS
    holder = jnp.sum(jnp.where(sectors == target, region_ids, 0)).astype(jnp.int32)
    moved = sectors[middle]
    sectors = sectors.at[holder].set(moved)
    sectors = sectors.at[middle].set(target)
    return sectors.astype(jnp.int32)


def block_scale(stream_key, dims, cuts, low, high):
    factor_of, own = 1.0, jax.random.fold_in(stream_key, 6)
    for position, shards_of in cuts:
        heights = jnp.exp(jax.random.uniform(jax.random.fold_in(own, position), (shards_of,), jnp.float32, low / len(cuts), high / len(cuts)))
        factor_of = factor_of * jnp.repeat(heights, dims[position] // shards_of).reshape([-1 if axis == position else 1 for axis in range(len(dims))])
    return factor_of


def centred(key, extent, scale, limit, pieces=(), held_as=jnp.bfloat16):
    array = scale * jax.random.normal(key, extent, jnp.float32)
    if pieces:
        array = array * block_scale(key, extent, pieces, -0.22, 0.18)
    return jnp.clip(array, -limit, limit).astype(held_as)


def setup_inputs(seed: int = 0) -> dict:
    key_list = jax.random.split(jax.random.key(seed), 6)
    return {
        "state_anom": centred(key_list[0], (REGIONS, LEVELS, COLS, MEMBERS), 1.0, 6.0, ((0, 8), (1, 4)), jnp.float32),
        "obs_anom": centred(key_list[1], (REGIONS, OBS_REG, MEMBERS), 1.0, 6.0, ((0, 8), (1, 4)), jnp.float32),
        "obs_weight": centred(key_list[2], (REGIONS, OBS_REG, MEMBERS), 1.0, 6.0, ((0, 8), (1, 4)), jnp.float32),
        "obs_cell": draw_obs_cell(jax.random.fold_in(key_list[5], 71), 0),
        "sector_of": draw_sector_of(jax.random.fold_in(key_list[5], 71), 0),
    }


def gaspari(scaled):
    inside = scaled * scaled * (scaled * (scaled * (0.5 - 0.25 * scaled) + 0.625) - 5.0 / 3.0) + 1.0
    floored = jnp.maximum(scaled, 1.0)
    outside = scaled * (scaled * (scaled * (scaled * (scaled / 12.0 - 0.5) + 0.625) + 5.0 / 3.0) - 5.0) + 4.0 - 2.0 / (3.0 * floored)
    return jnp.where(scaled <= 1.0, inside, jnp.where(scaled < 2.0, outside, 0.0))

def taper_tile(state_cells, obs_cells, lon_span):
    state_lon = state_cells // LAT
    state_lat = state_cells % LAT
    obs_lon = obs_cells // LAT
    obs_lat = obs_cells % LAT
    lon_gap = state_lon[:, None] - obs_lon[None, :]
    lon_gap = (lon_gap + lon_span + lon_span // 2) % lon_span - lon_span // 2
    lat_gap = state_lat[:, None] - obs_lat[None, :]
    scaled = jnp.sqrt((lon_gap * lon_gap + lat_gap * lat_gap).astype(jnp.float32)) / HALF
    return gaspari(scaled)

def neighbour(sector_of, region_ids, offset):
    target = (sector_of + offset + N_REGION) % N_REGION
    match = sector_of[None, :] == target[:, None]
    return lax.optimization_barrier(jnp.sum(jnp.where(match, region_ids[None, :], 0), axis=1)).astype(jnp.int32)

def reference(state_anom, obs_anom, obs_weight, obs_cell, sector_of):
    region_ids = jnp.arange(N_REGION, dtype=jnp.int32)
    lon_span = N_REGION * SECT_W
    left_of = neighbour(sector_of, region_ids, -1)
    right_of = neighbour(sector_of, region_ids, 1)
    global_cells = obs_cell + (sector_of * (SECT_W * LAT))[:, None]
    anom_blocks = obs_anom.reshape(N_REGION, N_STATE, OBS_DEV, MEMBERS)
    weight_blocks = obs_weight.reshape(N_REGION, N_STATE, OBS_DEV, MEMBERS)
    cell_blocks = global_cells.reshape(N_REGION, N_STATE, OBS_DEV)
    low_anom = anom_blocks[:, :, :CAP].reshape(N_REGION, N_STATE * CAP, MEMBERS)
    high_anom = anom_blocks[:, :, OBS_DEV - CAP:].reshape(N_REGION, N_STATE * CAP, MEMBERS)
    low_weight = weight_blocks[:, :, :CAP].reshape(N_REGION, N_STATE * CAP, MEMBERS)
    high_weight = weight_blocks[:, :, OBS_DEV - CAP:].reshape(N_REGION, N_STATE * CAP, MEMBERS)
    low_cells = cell_blocks[:, :, :CAP].reshape(N_REGION, N_STATE * CAP)
    high_cells = cell_blocks[:, :, OBS_DEV - CAP:].reshape(N_REGION, N_STATE * CAP)

    def one_region(index):
        left_region = left_of[index]
        right_region = right_of[index]
        anoms = jnp.concatenate([obs_anom[index], high_anom[left_region], low_anom[right_region]], axis=0)
        weights = jnp.concatenate([obs_weight[index], high_weight[left_region], low_weight[right_region]], axis=0)
        cells = jnp.concatenate([global_cells[index], high_cells[left_region], low_cells[right_region]], axis=0)
        state_cells = sector_of[index] * (SECT_W * LAT) + jnp.arange(COLS, dtype=jnp.int32)
        flat_state = state_anom[index].reshape(LEVELS * COLS, MEMBERS)
        covar = jnp.einsum('rm,pm->rp', flat_state, anoms, precision=lax.Precision.HIGHEST)
        tile = taper_tile(state_cells, cells, lon_span) / (MEMBERS - 1)
        covar = (covar.reshape(LEVELS, COLS, -1) * tile[None]).reshape(LEVELS * COLS, -1)
        result = jnp.dot(covar, weights, precision=lax.Precision.HIGHEST)
        return result.reshape(LEVELS, COLS, MEMBERS)
    return lax.map(one_region, region_ids)
```

```python
import functools

import jax
import jax.numpy as jnp
from jax import lax
from jax.experimental import pallas as pl
from jax.experimental.pallas import tpu as pltpu
from jax.sharding import PartitionSpec as P

SECT_W = 32
LAT = 8
HALF = 4
CAP = 16
COLS = 256
EDGE = 2 * HALF * LAT
SUB = 8
LANES = 128
VMEM = pl.BlockSpec(memory_space=pltpu.VMEM)
SMEM = pl.BlockSpec(memory_space=pltpu.SMEM)
ANY = pl.BlockSpec(memory_space=pl.ANY)


def partner(index, step, size):
    return index ^ step if size & (size - 1) == 0 else (index + size - step) % size


def target(index, step, size):
    return index ^ step if size & (size - 1) == 0 else (index + step) % size


def exchange(value, axis, step):
    size = lax.axis_size(axis)
    return lax.ppermute(value, axis, [(i, target(i, step, size)) for i in range(size)])


def gaspari(scaled):
    inside = scaled * scaled * (scaled * (scaled * (0.5 - 0.25 * scaled) + 0.625) - 5.0 / 3.0) + 1.0
    floored = jnp.maximum(scaled, 1.0)
    outside = (
        scaled * (scaled * (scaled * (scaled * (scaled / 12.0 - 0.5) + 0.625) + 5.0 / 3.0) - 5.0)
        + 4.0
        - 2.0 / (3.0 * floored)
    )
    return jnp.where(scaled <= 1.0, inside, jnp.where(scaled < 2.0, outside, 0.0))


def taper(first_col, rows, cells, lon_shift):
    cols = first_col + lax.broadcasted_iota(jnp.int32, (rows, cells.shape[1]), 0)
    obs = cells.astype(jnp.int32)
    lon_gap = cols // LAT - (obs // LAT + lon_shift)
    lat_gap = cols % LAT - obs % LAT
    scaled = jnp.sqrt((lon_gap * lon_gap + lat_gap * lat_gap).astype(jnp.float32)) / HALF
    return gaspari(scaled)


def split(value):
    high = value.astype(jnp.bfloat16)
    return high, (value - high.astype(jnp.float32)).astype(jnp.bfloat16)


def product(left, right, dims):
    dot = functools.partial(lax.dot_general, dimension_numbers=(dims, ((), ())), preferred_element_type=jnp.float32)
    return dot(left[0], right[0]) + (dot(left[0], right[1]) + dot(left[1], right[0]))


NT = ((1,), (1,))
NN = ((1,), (0,))


def folded(rows):
    return jnp.concatenate([rows[i : i + SUB] for i in range(0, rows.shape[0], SUB)], axis=1)


def unfolded(tiles, members):
    return jnp.concatenate([tiles[:, i : i + members] for i in range(0, tiles.shape[1], members)], axis=0)


def pack_kernel(sector_ref, anom_ref, weight_ref, cell_ref, own_ref, *slot_refs):
    regions = lax.axis_size("region")
    me = lax.axis_index("region")
    count = weight_ref.shape[0]
    members = weight_ref.shape[1]
    mine = sector_ref[me]
    left, right = jnp.int32(0), jnp.int32(0)
    for q in range(regions):
        sector = sector_ref[q]
        left = jnp.where(sector == lax.rem(mine + regions - 1, regions), q, left)
        right = jnp.where(sector == lax.rem(mine + 1, regions), q, right)
    cells = jnp.broadcast_to(cell_ref[...].astype(jnp.float32), (SUB, count)).astype(jnp.bfloat16)
    entry = lax.broadcasted_iota(jnp.int32, (count, LANES), 0)
    lane = lax.broadcasted_iota(jnp.int32, (count, LANES), 1)

    def spread(start, width):
        pick = jnp.where(entry == start + lane % width, 1.0, 0.0).astype(jnp.bfloat16)
        return lax.dot_general(cells, pick, (NN, ((), ())), preferred_element_type=jnp.float32)

    own_ref[:, : count // SUB * members] = folded(weight_ref[...])
    own_ref[:, count // SUB * members :] = spread(0, count)
    low = (folded(anom_ref[:CAP, :]), folded(weight_ref[:CAP, :]), spread(0, CAP))
    high = (folded(anom_ref[count - CAP :, :]), folded(weight_ref[count - CAP :, :]), spread(count - CAP, CAP))
    wide = CAP // SUB * members
    for step, slot in enumerate(slot_refs, start=1):
        to_right = target(me, step, regions) == right
        for (start, stop), lo, hi in zip(((0, wide), (wide, 2 * wide), (2 * wide, 2 * wide + LANES)), low, high):
            slot[:, start:stop] = jnp.where(to_right, hi, lo)


def pick_kernel(sector_ref, *refs):
    *slot_refs, halo_ref = refs
    regions = lax.axis_size("region")
    me = lax.axis_index("region")
    mine = sector_ref[me]
    width = slot_refs[0].shape[1]
    for step, slot in enumerate(slot_refs, start=1):
        sector = sector_ref[partner(me, step, regions)]

        @pl.when(sector == lax.rem(mine + regions - 1, regions))
        def _():
            halo_ref[:, :width] = slot[...]

        @pl.when(sector == lax.rem(mine + 1, regions))
        def _():
            halo_ref[:, width:] = slot[...]


def own_kernel(blocks, state_ref, *refs):
    anom_refs, pack_refs, (out_ref, a_hi, a_lo, w_hi, w_lo, rho_ref) = refs[:blocks], refs[blocks : 2 * blocks], refs[2 * blocks :]
    count, members = anom_refs[0].shape
    rows = state_ref.shape[0]

    @pl.when(pl.program_id(0) == 0)
    def _():
        lane = lax.broadcasted_iota(jnp.int32, (1, LANES), 1)
        tiles = [pack[:1, count // SUB * members :] for pack in pack_refs]
        for b in range(blocks):
            here = pl.ds(b * count, count)
            a_hi[here, :], a_lo[here, :] = split(anom_refs[b][...])
            w_hi[here, :], w_lo[here, :] = split(unfolded(pack_refs[b][:, : count // SUB * members], members))
        each = LANES // count
        for g in range(0, blocks, each):
            cells = tiles[g]
            for b in range(1, each):
                cells = jnp.where(lane >= b * count, tiles[g + b], cells)
            rho_ref[:, g * count : g * count + LANES] = taper(0, rows, cells, 0) / (members - 1)

    covar = product(split(state_ref[...]), (a_hi[...], a_lo[...]), NT) * rho_ref[...]
    out_ref[...] = product(split(covar), (w_hi[...], w_lo[...]), NN)


def halo_kernel(blocks, total_ref, state_ref, *refs):
    halo_refs, (out_ref, total_buf, state_buf, in_sem, state_sem, out_sem) = refs[:blocks], refs[blocks:]
    levels, columns, members = state_ref.shape
    wide = CAP // SUB * members
    width = halo_refs[0].shape[1] // 2
    starts = (0, columns - EDGE)
    loads = [
        (
            pltpu.make_async_copy(total_ref.at[l, pl.ds(c, EDGE)], total_buf.at[s, pl.ds(l * EDGE, EDGE)], in_sem.at[s, l]),
            pltpu.make_async_copy(state_ref.at[l, pl.ds(c, EDGE)], state_buf.at[s, pl.ds(l * EDGE, EDGE)], state_sem.at[s, l]),
        )
        for s, c in enumerate(starts)
        for l in range(levels)
    ]
    for total_load, state_load in loads:
        state_load.start()
        total_load.start()
    lane = lax.broadcasted_iota(jnp.int32, (1, LANES), 1)
    per = LANES // CAP
    parts = []
    for s, shift in enumerate((-SECT_W, SECT_W)):
        at = s * width
        anom = split(jnp.concatenate([unfolded(h[:, at : at + wide], members) for h in halo_refs], axis=0))
        weight = split(jnp.concatenate([unfolded(h[:, at + wide : at + 2 * wide], members) for h in halo_refs], axis=0))
        tiles = [h[:1, at + 2 * wide : at + width] for h in halo_refs]
        groups = []
        for g in range(0, blocks, per):
            cells = tiles[g]
            for b in range(1, min(per, blocks - g)):
                cells = jnp.where(lane >= b * CAP, tiles[g + b], cells)
            groups.append(cells)
        cells = jnp.concatenate(groups, axis=1)[:, : blocks * CAP]
        parts.append((anom, weight, taper(starts[s], EDGE, cells, shift) / (members - 1)))
    for _, state_load in loads:
        state_load.wait()
    deltas = []
    for s, (anom, weight, rho) in enumerate(parts):
        covar = product(split(state_buf[s]), anom, NT)
        covar = (covar.reshape(levels, EDGE, -1) * rho[None]).reshape(levels * EDGE, -1)
        deltas.append(product(split(covar), weight, NN))
    stores = []
    for s, c in enumerate(starts):
        for l in range(levels):
            loads[s * levels + l][0].wait()
        total_buf[s] += deltas[s]
        for l in range(levels):
            stores.append(
                pltpu.make_async_copy(total_buf.at[s, pl.ds(l * EDGE, EDGE)], out_ref.at[l, pl.ds(c, EDGE)], out_sem.at[s, l])
            )
            stores[-1].start()
    for store in stores:
        store.wait()


def on_device(state_anom, obs_anom, obs_weight, obs_cell, sector_of):
    f32 = jnp.float32
    regions, owners = lax.axis_size("region"), lax.axis_size("state")
    levels, columns, members = state_anom.shape[1:]
    own_anom, own_weight = obs_anom[0], obs_weight[0]
    count = own_anom.shape[0]
    blocks = owners

    anoms = [own_anom] + [exchange(own_anom, "state", k) for k in range(1, owners)]

    slot = jax.ShapeDtypeStruct((SUB, 2 * (CAP // SUB) * members + LANES), f32)
    own_pack, *slots = pl.pallas_call(
        pack_kernel,
        out_shape=[jax.ShapeDtypeStruct((SUB, count // SUB * members + LANES), f32)] + [slot] * (regions - 1),
        in_specs=[SMEM, VMEM, VMEM, VMEM],
        out_specs=[VMEM] * regions,
        name="pack",
    )(sector_of, own_anom, own_weight, obs_cell)
    got = [exchange(slots[k - 1], "region", k) for k in range(1, regions)]
    packs = [own_pack] + [exchange(own_pack, "state", k) for k in range(1, owners)]
    halo = pl.pallas_call(
        pick_kernel,
        out_shape=jax.ShapeDtypeStruct((SUB, 2 * slot.shape[1]), f32),
        in_specs=[SMEM] + [VMEM] * (regions - 1),
        out_specs=VMEM,
        name="pick",
    )(sector_of, *got)
    halos = [halo] + [exchange(halo, "state", k) for k in range(1, owners)]

    obs = blocks * count
    whole = lambda a: pl.BlockSpec(a.shape, lambda l: (0,) * a.ndim)
    level = pl.BlockSpec((None, columns, members), lambda l: (l, 0, 0))
    state = state_anom[0]
    bf16 = jnp.bfloat16
    total = pl.pallas_call(
        functools.partial(own_kernel, blocks),
        out_shape=jax.ShapeDtypeStruct(state.shape, f32),
        grid=(levels,),
        in_specs=[level] + [whole(a) for a in anoms + packs],
        out_specs=level,
        scratch_shapes=[pltpu.VMEM((obs, members), bf16)] * 4 + [pltpu.VMEM((columns, obs), f32)],
        cost_estimate=pl.CostEstimate(
            flops=12 * levels * columns * obs * members, bytes_accessed=8 * state.size + 8 * obs * members, transcendentals=0
        ),
        name="own",
    )(state, *anoms, *packs)
    out = pl.pallas_call(
        functools.partial(halo_kernel, blocks),
        out_shape=jax.ShapeDtypeStruct(state.shape, f32),
        in_specs=[ANY, ANY] + [VMEM] * blocks,
        out_specs=ANY,
        scratch_shapes=[pltpu.VMEM((2, levels * EDGE, members), f32)] * 2 + [pltpu.SemaphoreType.DMA((2, levels))] * 3,
        input_output_aliases={0: 0},
        name="halo",
    )(total, state, *halos)
    return out[None]


def solution(mesh):
    in_specs = (
        P("region", "state", None, None),
        P("region", "state", None),
        P("region", "state", None),
        P("region", "state"),
        P(),
    )
    out_specs = P("region", "state", None, None)
    return jax.shard_map(on_device, mesh=mesh, in_specs=in_specs, out_specs=out_specs, check_vma=False)
```

```python
import functools

import jax
import jax.numpy as jnp
from jax import lax
from jax.experimental import pallas as pl
from jax.experimental.pallas import tpu as pltpu
from jax.sharding import PartitionSpec as P

SECT_W = 32
LAT = 8
HALF = 4
CAP = 16
COLS = 256
EDGE = 2 * HALF * LAT
SUB = 8
LANES = 128
VMEM = pl.BlockSpec(memory_space=pltpu.VMEM)
SMEM = pl.BlockSpec(memory_space=pltpu.SMEM)
HBM = pl.BlockSpec(memory_space=pltpu.HBM)


def limit(mib):
    return pltpu.CompilerParams(vmem_limit_bytes=mib << 20)


def in_hbm(*values):
    return [pltpu.with_memory_space_constraint(value, pltpu.HBM) for value in values]


def partner(index, step, size):
    return index ^ step if size & (size - 1) == 0 else (index + size - step) % size


def target(index, step, size):
    return index ^ step if size & (size - 1) == 0 else (index + step) % size


def exchange(value, axis, step):
    size = lax.axis_size(axis)
    return lax.ppermute(value, axis, [(i, target(i, step, size)) for i in range(size)])


def gaspari(scaled):
    inside = scaled * scaled * (scaled * (scaled * (0.5 - 0.25 * scaled) + 0.625) - 5.0 / 3.0) + 1.0
    floored = jnp.maximum(scaled, 1.0)
    outside = (
        scaled * (scaled * (scaled * (scaled * (scaled / 12.0 - 0.5) + 0.625) + 5.0 / 3.0) - 5.0)
        + 4.0
        - 2.0 / (3.0 * floored)
    )
    return jnp.where(scaled <= 1.0, inside, jnp.where(scaled < 2.0, outside, 0.0))


def taper(first_col, rows, cells, lon_shift):
    cols = first_col + lax.broadcasted_iota(jnp.int32, (rows, cells.shape[1]), 0)
    obs = cells.astype(jnp.int32)
    lon_gap = cols // LAT - (obs // LAT + lon_shift)
    lat_gap = cols % LAT - obs % LAT
    scaled = jnp.sqrt((lon_gap * lon_gap + lat_gap * lat_gap).astype(jnp.float32)) / HALF
    return gaspari(scaled)


def split(value):
    high = value.astype(jnp.bfloat16)
    return high, (value - high.astype(jnp.float32)).astype(jnp.bfloat16)


def product(left, right, dims):
    dot = functools.partial(lax.dot_general, dimension_numbers=(dims, ((), ())), preferred_element_type=jnp.float32)
    return dot(left[0], right[0]) + (dot(left[0], right[1]) + dot(left[1], right[0]))


NT = ((1,), (1,))
NN = ((1,), (0,))


def folded(rows):
    return jnp.concatenate([rows[i : i + SUB] for i in range(0, rows.shape[0], SUB)], axis=1)


def unfolded(tiles, members):
    return jnp.concatenate([tiles[:, i : i + members] for i in range(0, tiles.shape[1], members)], axis=0)


def pack_kernel(sector_hbm, anom_hbm, weight_hbm, cell_hbm, own_ref, *refs):
    side_ref, *slot_refs, sector_ref, anom_ref, weight_ref, cell_ref, sems = refs
    count, members = weight_ref.shape
    loads = [
        pltpu.make_async_copy(cell_hbm, cell_ref, sems.at[0]),
        pltpu.make_async_copy(sector_hbm, sector_ref, sems.at[1]),
        pltpu.make_async_copy(weight_hbm.at[0], weight_ref, sems.at[2]),
        pltpu.make_async_copy(anom_hbm.at[0, pl.ds(0, CAP)], anom_ref.at[pl.ds(0, CAP)], sems.at[3]),
        pltpu.make_async_copy(anom_hbm.at[0, pl.ds(count - CAP, CAP)], anom_ref.at[pl.ds(CAP, CAP)], sems.at[4]),
    ]
    for load in loads:
        load.start()
    regions = lax.axis_size("region")
    me = lax.axis_index("region")
    entry = lax.broadcasted_iota(jnp.int32, (count, LANES), 0)
    lane = lax.broadcasted_iota(jnp.int32, (count, LANES), 1)
    picks = [
        jnp.where(entry == start + lane % width, 1.0, 0.0).astype(jnp.bfloat16)
        for start, width in ((0, count), (0, CAP), (count - CAP, CAP))
    ]
    loads[0].wait()
    cells = jnp.broadcast_to(cell_ref[...].astype(jnp.float32), (SUB, count)).astype(jnp.bfloat16)
    spread = [lax.dot_general(cells, pick, (NN, ((), ())), preferred_element_type=jnp.float32) for pick in picks]
    loads[1].wait()
    mine = sector_ref[me]
    to_right, from_left, from_right = [], jnp.int32(0), jnp.int32(0)
    for step in range(1, regions):
        to_right.append(sector_ref[target(me, step, regions)] == lax.rem(mine + 1, regions))
        sector = sector_ref[partner(me, step, regions)]
        from_left = jnp.where(sector == lax.rem(mine + regions - 1, regions), step, from_left)
        from_right = jnp.where(sector == lax.rem(mine + 1, regions), step, from_right)
    side_ref[0] = jnp.broadcast_to(from_left, (SUB, LANES))
    side_ref[1] = jnp.broadcast_to(from_right, (SUB, LANES))
    for load in loads[2:]:
        load.wait()
    own_ref[:, : count // SUB * members] = folded(weight_ref[...])
    own_ref[:, count // SUB * members :] = spread[0]
    low = (folded(anom_ref[:CAP, :]), folded(weight_ref[:CAP, :]), spread[1])
    high = (folded(anom_ref[CAP:, :]), folded(weight_ref[count - CAP :, :]), spread[2])
    wide = CAP // SUB * members
    for slot, up in zip(slot_refs, to_right):
        for (start, stop), lo, hi in zip(((0, wide), (wide, 2 * wide), (2 * wide, 2 * wide + LANES)), low, high):
            slot[:, start:stop] = jnp.where(up, hi, lo)


def pick_kernel(side_ref, *refs):
    *slot_refs, halo_ref = refs
    width = slot_refs[0].shape[1]
    for side in range(2):
        step_of = side_ref[side]
        for at in range(0, width, LANES):
            value = slot_refs[0][:, at : at + LANES]
            for step, slot in enumerate(slot_refs[1:], start=2):
                value = jnp.where(step_of == step, slot[:, at : at + LANES], value)
            halo_ref[:, side * width + at : side * width + at + LANES] = value


def own_kernel(blocks, state_hbm, anom_hbm, *refs):
    anom_refs, pack_refs = refs[: blocks - 1], refs[blocks - 1 : 2 * blocks - 1]
    out_hbm, state_ref, anom_ref, out_ref, a_hi, a_lo, w_hi, w_lo, rho_ref, in_sem, out_sem = refs[2 * blocks - 1 :]
    anom_refs = (*anom_refs, anom_ref)
    pack_refs = (*pack_refs[1:], pack_refs[0])
    count, members = anom_refs[0].shape
    levels, rows = state_ref.shape[:2]
    loads = [pltpu.make_async_copy(state_hbm.at[l], state_ref.at[l], in_sem.at[l]) for l in range(levels)]
    loads.append(pltpu.make_async_copy(anom_hbm, anom_ref, in_sem.at[levels]))
    for load in loads[::-1]:
        load.start()
    lane = lax.broadcasted_iota(jnp.int32, (1, LANES), 1)
    tiles = [pack[:1, count // SUB * members :] for pack in pack_refs]
    for b in range(blocks):
        here = pl.ds(b * count, count)
        if b == blocks - 1:
            loads[levels].wait()
        a_hi[here, :], a_lo[here, :] = split(anom_refs[b][...])
        w_hi[here, :], w_lo[here, :] = split(unfolded(pack_refs[b][:, : count // SUB * members], members))
    each = LANES // count
    for g in range(0, blocks, each):
        cells = tiles[g]
        for b in range(1, each):
            cells = jnp.where(lane >= b * count, tiles[g + b], cells)
        rho_ref[:, g * count : g * count + LANES] = taper(0, rows, cells, 0) / (members - 1)
    stores = []
    for l in range(levels):
        loads[l].wait()
        covar = product(split(state_ref[l]), (a_hi[...], a_lo[...]), NT) * rho_ref[...]
        out_ref[l] = product(split(covar), (w_hi[...], w_lo[...]), NN)
        stores.append(pltpu.make_async_copy(out_ref.at[l], out_hbm.at[l], out_sem.at[l]))
        stores[-1].start()
    for store in stores:
        store.wait()


def halo_kernel(blocks, total_ref, state_ref, *refs):
    halo_refs, (out_ref, total_buf, state_buf, in_sem, state_sem, out_sem) = refs[:blocks], refs[blocks:]
    levels, columns, members = state_ref.shape
    wide = CAP // SUB * members
    width = halo_refs[0].shape[1] // 2
    starts = (0, columns - EDGE)
    loads = [
        (
            pltpu.make_async_copy(total_ref.at[l, pl.ds(c, EDGE)], total_buf.at[s, pl.ds(l * EDGE, EDGE)], in_sem.at[s, l]),
            pltpu.make_async_copy(state_ref.at[l, pl.ds(c, EDGE)], state_buf.at[s, pl.ds(l * EDGE, EDGE)], state_sem.at[s, l]),
        )
        for s, c in enumerate(starts)
        for l in range(levels)
    ]
    for total_load, state_load in loads:
        state_load.start()
        total_load.start()
    lane = lax.broadcasted_iota(jnp.int32, (1, LANES), 1)
    per = LANES // CAP
    parts = []
    for s, shift in enumerate((-SECT_W, SECT_W)):
        at = s * width
        anom = split(jnp.concatenate([unfolded(h[:, at : at + wide], members) for h in halo_refs], axis=0))
        weight = split(jnp.concatenate([unfolded(h[:, at + wide : at + 2 * wide], members) for h in halo_refs], axis=0))
        tiles = [h[:1, at + 2 * wide : at + width] for h in halo_refs]
        groups = []
        for g in range(0, blocks, per):
            cells = tiles[g]
            for b in range(1, min(per, blocks - g)):
                cells = jnp.where(lane >= b * CAP, tiles[g + b], cells)
            groups.append(cells)
        cells = jnp.concatenate(groups, axis=1)[:, : blocks * CAP]
        parts.append((anom, weight, taper(starts[s], EDGE, cells, shift) / (members - 1)))
    for _, state_load in loads:
        state_load.wait()
    deltas = []
    for s, (anom, weight, rho) in enumerate(parts):
        covar = product(split(state_buf[s]), anom, NT)
        covar = (covar.reshape(levels, EDGE, -1) * rho[None]).reshape(levels * EDGE, -1)
        deltas.append(product(split(covar), weight, NN))
    stores = []
    for s, c in enumerate(starts):
        for l in range(levels):
            loads[s * levels + l][0].wait()
        total_buf[s] += deltas[s]
        for l in range(levels):
            stores.append(
                pltpu.make_async_copy(total_buf.at[s, pl.ds(l * EDGE, EDGE)], out_ref.at[l, pl.ds(c, EDGE)], out_sem.at[s, l])
            )
            stores[-1].start()
    for store in stores:
        store.wait()


def on_device(state_anom, obs_anom, obs_weight, obs_cell, sector_of):
    f32 = jnp.float32
    regions, owners = lax.axis_size("region"), lax.axis_size("state")
    levels, columns, members = state_anom.shape[1:]
    own_anom, own_weight = obs_anom[0], obs_weight[0]
    count = own_anom.shape[0]
    blocks = owners

    anoms = [own_anom] + [exchange(own_anom, "state", k) for k in range(1, owners)]

    slot = jax.ShapeDtypeStruct((SUB, 2 * (CAP // SUB) * members + LANES), f32)
    own_pack, sides, *slots = pl.pallas_call(
        pack_kernel,
        out_shape=[jax.ShapeDtypeStruct((SUB, count // SUB * members + LANES), f32)]
        + [jax.ShapeDtypeStruct((2, SUB, LANES), jnp.int32)]
        + [slot] * (regions - 1),
        in_specs=[HBM] * 4,
        out_specs=[VMEM] * (regions + 1),
        scratch_shapes=[
            pltpu.SMEM((regions,), jnp.int32),
            pltpu.VMEM((2 * CAP, members), f32),
            pltpu.VMEM((count, members), f32),
            pltpu.VMEM((1, count), jnp.int32),
            pltpu.SemaphoreType.DMA((5,)),
        ],
        compiler_params=limit(8),
        name="pack",
    )(*in_hbm(sector_of, obs_anom, obs_weight, obs_cell))
    got = [exchange(slots[k - 1], "region", k) for k in range(1, regions)]
    packs = [own_pack] + [exchange(own_pack, "state", k) for k in range(1, owners)]
    halo = pl.pallas_call(
        pick_kernel,
        out_shape=jax.ShapeDtypeStruct((SUB, 2 * slot.shape[1]), f32),
        in_specs=[VMEM] * regions,
        out_specs=VMEM,
        compiler_params=limit(4),
        name="pick",
    )(sides, *got)
    halos = [halo] + [exchange(halo, "state", k) for k in range(1, owners)]

    obs = blocks * count
    state = state_anom[0]
    bf16 = jnp.bfloat16
    total = pl.pallas_call(
        functools.partial(own_kernel, blocks),
        out_shape=jax.ShapeDtypeStruct(state.shape, f32),
        in_specs=[HBM] * 2 + [VMEM] * (2 * blocks - 1),
        out_specs=HBM,
        scratch_shapes=[pltpu.VMEM(state.shape, f32), pltpu.VMEM(own_anom.shape, f32), pltpu.VMEM(state.shape, f32)]
        + [pltpu.VMEM((obs, members), bf16)] * 4
        + [pltpu.VMEM((columns, obs), f32)]
        + [pltpu.SemaphoreType.DMA((levels + 1,)), pltpu.SemaphoreType.DMA((levels,))],
        cost_estimate=pl.CostEstimate(
            flops=12 * levels * columns * obs * members, bytes_accessed=8 * state.size + 8 * obs * members, transcendentals=0
        ),
        compiler_params=limit(24),
        name="own",
    )(*in_hbm(state, own_anom), *anoms[1:], *packs)
    out = pl.pallas_call(
        functools.partial(halo_kernel, blocks),
        out_shape=jax.ShapeDtypeStruct(state.shape, f32),
        in_specs=[HBM, HBM] + [VMEM] * blocks,
        out_specs=HBM,
        scratch_shapes=[pltpu.VMEM((2, levels * EDGE, members), f32)] * 2 + [pltpu.SemaphoreType.DMA((2, levels))] * 3,
        input_output_aliases={0: 0},
        compiler_params=limit(16),
        name="halo",
    )(total, *in_hbm(state), *halos)
    return out[None]


def solution(mesh):
    in_specs = (
        P("region", "state", None, None),
        P("region", "state", None),
        P("region", "state", None),
        P("region", "state"),
        P(),
    )
    out_specs = P("region", "state", None, None)
    return jax.shard_map(on_device, mesh=mesh, in_specs=in_specs, out_specs=out_specs, check_vma=False)
```

```python
import functools

import jax
import jax.numpy as jnp
from jax import lax
from jax.experimental import pallas as pl
from jax.experimental.pallas import tpu as pltpu
from jax.sharding import PartitionSpec as P


SECT_W = 32
LAT = 8
HALF = 4
CAP = 16
EDGE = 2 * HALF * LAT
SUB = 8
LANES = 128
VMEM = pl.BlockSpec(memory_space=pltpu.VMEM)
SMEM = pl.BlockSpec(memory_space=pltpu.SMEM)
HBM = pl.BlockSpec(memory_space=pltpu.HBM)


def limit(mib):
    return pltpu.CompilerParams(vmem_limit_bytes=mib << 20)


def in_hbm(*values):
    return [pltpu.with_memory_space_constraint(value, pltpu.HBM) for value in values]


def partner(index, step, size):
    return index ^ step if size & (size - 1) == 0 else (index + size - step) % size


def target(index, step, size):
    return index ^ step if size & (size - 1) == 0 else (index + step) % size


def exchange(value, axis, step):
    size = lax.axis_size(axis)
    return lax.ppermute(value, axis, [(i, target(i, step, size)) for i in range(size)])


def gaspari(scaled):
    inside = scaled * scaled * (scaled * (scaled * (0.5 - 0.25 * scaled) + 0.625) - 5.0 / 3.0) + 1.0
    floored = jnp.maximum(scaled, 1.0)
    outside = (
        scaled * (scaled * (scaled * (scaled * (scaled / 12.0 - 0.5) + 0.625) + 5.0 / 3.0) - 5.0)
        + 4.0
        - 2.0 / (3.0 * floored)
    )
    return jnp.where(scaled <= 1.0, inside, jnp.where(scaled < 2.0, outside, 0.0))


def taper(first_col, rows, cells, lon_shift):
    cols = first_col + lax.broadcasted_iota(jnp.int32, (rows, cells.shape[1]), 0)
    obs = cells.astype(jnp.int32)
    lon_gap = cols // LAT - (obs // LAT + lon_shift)
    lat_gap = cols % LAT - obs % LAT
    scaled = jnp.sqrt((lon_gap * lon_gap + lat_gap * lat_gap).astype(jnp.float32)) / HALF
    return gaspari(scaled)


def split(value):
    high = value.astype(jnp.bfloat16)
    return high, (value - high.astype(jnp.float32)).astype(jnp.bfloat16)


def product(left, right, dims):
    dot = functools.partial(lax.dot_general, dimension_numbers=(dims, ((), ())), preferred_element_type=jnp.float32)
    return dot(left[0], right[0]) + (dot(left[0], right[1]) + dot(left[1], right[0]))


NT = ((1,), (1,))
NN = ((1,), (0,))


def folded(rows):
    return jnp.concatenate([rows[i : i + SUB] for i in range(0, rows.shape[0], SUB)], axis=1)


def unfolded(tiles, members):
    return jnp.concatenate([tiles[:, i : i + members] for i in range(0, tiles.shape[1], members)], axis=0)


def pack_kernel(sector_hbm, anom_hbm, weight_hbm, cell_hbm, own_ref, *refs):
    side_ref, *slot_refs, sector_ref, anom_ref, weight_ref, cell_ref, sems = refs
    count, members = weight_ref.shape
    loads = [
        pltpu.make_async_copy(cell_hbm, cell_ref, sems.at[0]),
        pltpu.make_async_copy(sector_hbm, sector_ref, sems.at[1]),
        pltpu.make_async_copy(weight_hbm.at[0], weight_ref, sems.at[2]),
        pltpu.make_async_copy(anom_hbm.at[0], anom_ref, sems.at[3]),
    ]
    for load in loads:
        load.start()
    regions = lax.axis_size("region")
    me = lax.axis_index("region")
    entry = lax.broadcasted_iota(jnp.int32, (count, LANES), 0)
    lane = lax.broadcasted_iota(jnp.int32, (count, LANES), 1)
    picks = [
        jnp.where(entry == start + lane % width, 1.0, 0.0).astype(jnp.bfloat16)
        for start, width in ((0, count), (0, CAP), (count - CAP, CAP))
    ]
    loads[0].wait()
    cells = jnp.broadcast_to(cell_ref[...].astype(jnp.float32), (SUB, count)).astype(jnp.bfloat16)
    spread = [lax.dot_general(cells, pick, (NN, ((), ())), preferred_element_type=jnp.float32) for pick in picks]
    loads[1].wait()
    mine = sector_ref[me]
    to_right, from_left, from_right = [], jnp.int32(0), jnp.int32(0)
    for step in range(1, regions):
        to_right.append(sector_ref[target(me, step, regions)] == lax.rem(mine + 1, regions))
        sector = sector_ref[partner(me, step, regions)]
        from_left = jnp.where(sector == lax.rem(mine + regions - 1, regions), step, from_left)
        from_right = jnp.where(sector == lax.rem(mine + 1, regions), step, from_right)
    side_ref[0] = jnp.broadcast_to(from_left, (SUB, LANES))
    side_ref[1] = jnp.broadcast_to(from_right, (SUB, LANES))
    for load in loads[2:]:
        load.wait()
    half = count // SUB * members
    own_ref[:, :half] = folded(anom_ref[...])
    own_ref[:, half : 2 * half] = folded(weight_ref[...])
    own_ref[:, 2 * half :] = spread[0]
    low = (folded(anom_ref[:CAP, :]), folded(weight_ref[:CAP, :]), spread[1])
    high = (folded(anom_ref[count - CAP :, :]), folded(weight_ref[count - CAP :, :]), spread[2])
    wide = CAP // SUB * members
    for slot, up in zip(slot_refs, to_right):
        for (start, stop), lo, hi in zip(((0, wide), (wide, 2 * wide), (2 * wide, 2 * wide + LANES)), low, high):
            slot[:, start:stop] = jnp.where(up, hi, lo)


def pick_kernel(side_ref, *refs):
    *slot_refs, halo_ref = refs
    width = slot_refs[0].shape[1]
    for side in range(2):
        step_of = side_ref[side]
        for at in range(0, width, LANES):
            value = slot_refs[0][:, at : at + LANES]
            for step, slot in enumerate(slot_refs[1:], start=2):
                value = jnp.where(step_of == step, slot[:, at : at + LANES], value)
            halo_ref[:, side * width + at : side * width + at + LANES] = value


def own_kernel(blocks, state_hbm, *refs):
    pack_refs, (out_hbm, state_ref, out_ref, a_hi, a_lo, w_hi, w_lo, rho_ref, in_sem, out_sem) = refs[:blocks], refs[blocks:]
    levels, rows, members = state_ref.shape
    half = pack_refs[0].shape[1] // 2 // LANES * LANES
    count = half // members * SUB
    loads = [pltpu.make_async_copy(state_hbm.at[l], state_ref.at[l], in_sem.at[l]) for l in range(levels)]
    for load in loads:
        load.start()
    lane = lax.broadcasted_iota(jnp.int32, (1, LANES), 1)
    tiles = [pack[:1, 2 * half :] for pack in pack_refs]
    for b in range(blocks):
        here = pl.ds(b * count, count)
        a_hi[here, :], a_lo[here, :] = split(unfolded(pack_refs[b][:, :half], members))
        w_hi[here, :], w_lo[here, :] = split(unfolded(pack_refs[b][:, half : 2 * half], members))
    each = LANES // count
    for g in range(0, blocks, each):
        cells = tiles[g]
        for b in range(1, each):
            cells = jnp.where(lane >= b * count, tiles[g + b], cells)
        rho_ref[:, g * count : g * count + LANES] = taper(0, rows, cells, 0) / (members - 1)
    stores = []
    for l in range(levels):
        loads[l].wait()
        covar = product(split(state_ref[l]), (a_hi[...], a_lo[...]), NT) * rho_ref[...]
        out_ref[l] = product(split(covar), (w_hi[...], w_lo[...]), NN)
        stores.append(pltpu.make_async_copy(out_ref.at[l], out_hbm.at[l], out_sem.at[l]))
        stores[-1].start()
    for store in stores:
        store.wait()


def halo_kernel(blocks, total_ref, state_ref, *refs):
    halo_refs, (out_ref, total_buf, state_buf, in_sem, state_sem, out_sem) = refs[:blocks], refs[blocks:]
    levels, columns, members = state_ref.shape
    wide = CAP // SUB * members
    width = halo_refs[0].shape[1] // 2
    starts = (0, columns - EDGE)
    loads = [
        (
            pltpu.make_async_copy(total_ref.at[l, pl.ds(c, EDGE)], total_buf.at[s, pl.ds(l * EDGE, EDGE)], in_sem.at[s, l]),
            pltpu.make_async_copy(state_ref.at[l, pl.ds(c, EDGE)], state_buf.at[s, pl.ds(l * EDGE, EDGE)], state_sem.at[s, l]),
        )
        for s, c in enumerate(starts)
        for l in range(levels)
    ]
    for total_load, state_load in loads:
        state_load.start()
        total_load.start()
    lane = lax.broadcasted_iota(jnp.int32, (1, LANES), 1)
    per = LANES // CAP
    parts = []
    for s, shift in enumerate((-SECT_W, SECT_W)):
        at = s * width
        anom = split(jnp.concatenate([unfolded(h[:, at : at + wide], members) for h in halo_refs], axis=0))
        weight = split(jnp.concatenate([unfolded(h[:, at + wide : at + 2 * wide], members) for h in halo_refs], axis=0))
        tiles = [h[:1, at + 2 * wide : at + width] for h in halo_refs]
        groups = []
        for g in range(0, blocks, per):
            cells = tiles[g]
            for b in range(1, min(per, blocks - g)):
                cells = jnp.where(lane >= b * CAP, tiles[g + b], cells)
            groups.append(cells)
        cells = jnp.concatenate(groups, axis=1)[:, : blocks * CAP]
        parts.append((anom, weight, taper(starts[s], EDGE, cells, shift) / (members - 1)))
    for _, state_load in loads:
        state_load.wait()
    deltas = []
    for s, (anom, weight, rho) in enumerate(parts):
        covar = product(split(state_buf[s]), anom, NT)
        covar = (covar.reshape(levels, EDGE, -1) * rho[None]).reshape(levels * EDGE, -1)
        deltas.append(product(split(covar), weight, NN))
    stores = []
    for s, c in enumerate(starts):
        for l in range(levels):
            loads[s * levels + l][0].wait()
        total_buf[s] += deltas[s]
        for l in range(levels):
            stores.append(
                pltpu.make_async_copy(total_buf.at[s, pl.ds(l * EDGE, EDGE)], out_ref.at[l, pl.ds(c, EDGE)], out_sem.at[s, l])
            )
            stores[-1].start()
    for store in stores:
        store.wait()


def on_device(state_anom, obs_anom, obs_weight, obs_cell, sector_of):
    f32 = jnp.float32
    regions, owners = lax.axis_size("region"), lax.axis_size("state")
    levels, columns, members = state_anom.shape[1:]
    count = obs_anom.shape[1]
    blocks = owners

    slot = jax.ShapeDtypeStruct((SUB, 2 * (CAP // SUB) * members + LANES), f32)
    own_pack, sides, *slots = pl.pallas_call(
        pack_kernel,
        out_shape=[jax.ShapeDtypeStruct((SUB, 2 * (count // SUB) * members + LANES), f32)]
        + [jax.ShapeDtypeStruct((2, SUB, LANES), jnp.int32)]
        + [slot] * (regions - 1),
        in_specs=[HBM] * 4,
        out_specs=[VMEM] * (regions + 1),
        scratch_shapes=[
            pltpu.SMEM((regions,), jnp.int32),
            pltpu.VMEM((count, members), f32),
            pltpu.VMEM((count, members), f32),
            pltpu.VMEM((1, count), jnp.int32),
            pltpu.SemaphoreType.DMA((4,)),
        ],
        compiler_params=limit(8),
        name="pack",
    )(*in_hbm(sector_of, obs_anom, obs_weight, obs_cell))
    got = [exchange(slots[k - 1], "region", k) for k in range(1, regions)]
    packs = [own_pack] + [exchange(own_pack, "state", k) for k in range(1, owners)]
    halo = pl.pallas_call(
        pick_kernel,
        out_shape=jax.ShapeDtypeStruct((SUB, 2 * slot.shape[1]), f32),
        in_specs=[VMEM] * regions,
        out_specs=VMEM,
        compiler_params=limit(4),
        name="pick",
    )(sides, *got)
    halos = [halo] + [exchange(halo, "state", k) for k in range(1, owners)]

    obs = blocks * count
    state = state_anom[0]
    bf16 = jnp.bfloat16
    total = pl.pallas_call(
        functools.partial(own_kernel, blocks),
        out_shape=jax.ShapeDtypeStruct(state.shape, f32),
        in_specs=[HBM] + [VMEM] * blocks,
        out_specs=HBM,
        scratch_shapes=[pltpu.VMEM(state.shape, f32)] * 2
        + [pltpu.VMEM((obs, members), bf16)] * 4
        + [pltpu.VMEM((columns, obs), f32)]
        + [pltpu.SemaphoreType.DMA((levels,))] * 2,
        cost_estimate=pl.CostEstimate(
            flops=12 * levels * columns * obs * members, bytes_accessed=8 * state.size + 8 * obs * members, transcendentals=0
        ),
        compiler_params=limit(24),
        name="own",
    )(*in_hbm(state), *packs)
    out = pl.pallas_call(
        functools.partial(halo_kernel, blocks),
        out_shape=jax.ShapeDtypeStruct(state.shape, f32),
        in_specs=[HBM, HBM] + [VMEM] * blocks,
        out_specs=HBM,
        scratch_shapes=[pltpu.VMEM((2, levels * EDGE, members), f32)] * 2 + [pltpu.SemaphoreType.DMA((2, levels))] * 3,
        input_output_aliases={0: 0},
        compiler_params=limit(16),
        name="halo",
    )(total, *in_hbm(state), *halos)
    return out[None]


def solution(mesh):
    in_specs = (
        P("region", "state", None, None),
        P("region", "state", None),
        P("region", "state", None),
        P("region", "state"),
        P(),
    )
    out_specs = P("region", "state", None, None)
    return jax.shard_map(on_device, mesh=mesh, in_specs=in_specs, out_specs=out_specs, check_vma=False)
```

```python
import functools

import jax
import jax.numpy as jnp
from jax import lax
from jax.experimental import pallas as pl
from jax.experimental.pallas import tpu as pltpu
from jax.sharding import PartitionSpec as P


SECT_W = 32
LAT = 8
HALF = 4
CAP = 16
EDGE = 2 * HALF * LAT
SUB = 8
LANES = 128
VMEM = pl.BlockSpec(memory_space=pltpu.VMEM)
SMEM = pl.BlockSpec(memory_space=pltpu.SMEM)
HBM = pl.BlockSpec(memory_space=pltpu.HBM)


def limit(mib):
    return pltpu.CompilerParams(vmem_limit_bytes=mib << 20)


def in_hbm(*values):
    return [pltpu.with_memory_space_constraint(value, pltpu.HBM) for value in values]


def partner(index, step, size):
    return index ^ step if size & (size - 1) == 0 else (index + size - step) % size


def target(index, step, size):
    return index ^ step if size & (size - 1) == 0 else (index + step) % size


def exchange(value, axis, step):
    size = lax.axis_size(axis)
    return lax.ppermute(value, axis, [(i, target(i, step, size)) for i in range(size)])


def gaspari(scaled):
    inside = scaled * scaled * (scaled * (scaled * (0.5 - 0.25 * scaled) + 0.625) - 5.0 / 3.0) + 1.0
    floored = jnp.maximum(scaled, 1.0)
    outside = (
        scaled * (scaled * (scaled * (scaled * (scaled / 12.0 - 0.5) + 0.625) + 5.0 / 3.0) - 5.0)
        + 4.0
        - 2.0 / (3.0 * floored)
    )
    return jnp.where(scaled <= 1.0, inside, jnp.where(scaled < 2.0, outside, 0.0))


def taper(first_col, rows, cells, lon_shift):
    cols = first_col + lax.broadcasted_iota(jnp.int32, (rows, cells.shape[1]), 0)
    obs = cells.astype(jnp.int32)
    lon_gap = cols // LAT - (obs // LAT + lon_shift)
    lat_gap = cols % LAT - obs % LAT
    scaled = jnp.sqrt((lon_gap * lon_gap + lat_gap * lat_gap).astype(jnp.float32)) / HALF
    return gaspari(scaled)


def split(value):
    high = value.astype(jnp.bfloat16)
    return high, (value - high.astype(jnp.float32)).astype(jnp.bfloat16)


def product(left, right, dims):
    dot = functools.partial(lax.dot_general, dimension_numbers=(dims, ((), ())), preferred_element_type=jnp.float32)
    return dot(left[0], right[0]) + (dot(left[0], right[1]) + dot(left[1], right[0]))


NT = ((1,), (1,))
NN = ((1,), (0,))


def folded(rows):
    return jnp.concatenate([rows[i : i + SUB] for i in range(0, rows.shape[0], SUB)], axis=1)


def unfolded(tiles, members):
    return jnp.concatenate([tiles[:, i : i + members] for i in range(0, tiles.shape[1], members)], axis=0)


def pack_kernel(sector_hbm, anom_hbm, weight_hbm, cell_hbm, own_ref, *refs):
    side_ref, *slot_refs, sector_ref, anom_ref, weight_ref, cell_ref, sems = refs
    count, members = weight_ref.shape
    loads = [
        pltpu.make_async_copy(cell_hbm, cell_ref, sems.at[0]),
        pltpu.make_async_copy(sector_hbm, sector_ref, sems.at[1]),
        pltpu.make_async_copy(weight_hbm.at[0], weight_ref, sems.at[2]),
        pltpu.make_async_copy(anom_hbm.at[0], anom_ref, sems.at[3]),
    ]
    for load in loads:
        load.start()
    regions = lax.axis_size("region")
    me = lax.axis_index("region")
    entry = lax.broadcasted_iota(jnp.int32, (count, LANES), 0)
    lane = lax.broadcasted_iota(jnp.int32, (count, LANES), 1)
    picks = [
        jnp.where(entry == start + lane % width, 1.0, 0.0).astype(jnp.bfloat16)
        for start, width in ((0, count), (0, CAP), (count - CAP, CAP))
    ]
    loads[0].wait()
    cells = jnp.broadcast_to(cell_ref[...].astype(jnp.float32), (SUB, count)).astype(jnp.bfloat16)
    spread = [lax.dot_general(cells, pick, (NN, ((), ())), preferred_element_type=jnp.float32) for pick in picks]
    loads[1].wait()
    mine = sector_ref[me]
    to_right, from_left, from_right = [], jnp.int32(0), jnp.int32(0)
    for step in range(1, regions):
        to_right.append(sector_ref[target(me, step, regions)] == lax.rem(mine + 1, regions))
        sector = sector_ref[partner(me, step, regions)]
        from_left = jnp.where(sector == lax.rem(mine + regions - 1, regions), step, from_left)
        from_right = jnp.where(sector == lax.rem(mine + 1, regions), step, from_right)
    side_ref[0] = jnp.broadcast_to(from_left, (SUB, LANES))
    side_ref[1] = jnp.broadcast_to(from_right, (SUB, LANES))
    for load in loads[2:]:
        load.wait()
    half = count // SUB * members
    own_ref[:, :half] = folded(anom_ref[...])
    own_ref[:, half : 2 * half] = folded(weight_ref[...])
    own_ref[:, 2 * half :] = spread[0]
    low = (folded(anom_ref[:CAP, :]), folded(weight_ref[:CAP, :]), spread[1])
    high = (folded(anom_ref[count - CAP :, :]), folded(weight_ref[count - CAP :, :]), spread[2])
    wide = CAP // SUB * members
    for slot, up in zip(slot_refs, to_right):
        for (start, stop), lo, hi in zip(((0, wide), (wide, 2 * wide), (2 * wide, 2 * wide + LANES)), low, high):
            slot[:, start:stop] = jnp.where(up, hi, lo)


def pick_kernel(side_ref, *refs):
    *slot_refs, halo_ref = refs
    width = slot_refs[0].shape[1]
    for side in range(2):
        step_of = side_ref[side]
        for at in range(0, width, LANES):
            value = slot_refs[0][:, at : at + LANES]
            for step, slot in enumerate(slot_refs[1:], start=2):
                value = jnp.where(step_of == step, slot[:, at : at + LANES], value)
            halo_ref[:, side * width + at : side * width + at + LANES] = value


def joined(left, right, dims):
    axis = dims[1][0]
    lefts = jnp.concatenate([left[0], left[0], left[1]], axis=1)
    rights = jnp.concatenate([right[0], right[1], right[0]], axis=axis)
    return lax.dot_general(lefts, rights, (dims, ((), ())), preferred_element_type=jnp.float32)


def own_kernel(blocks, state_hbm, *refs):
    pack_refs, (out_hbm, edge_ref, s_hi, s_lo) = refs[:blocks], refs[blocks : blocks + 4]
    state_ref, out_ref, a_hi, a_lo, w_hi, w_lo, rho_ref, in_sem, out_sem = refs[blocks + 4 :]
    levels, rows, members = state_ref.shape
    half = pack_refs[0].shape[1] // 2 // LANES * LANES
    count = half // members * SUB
    loads = [pltpu.make_async_copy(state_hbm.at[l], state_ref.at[l], in_sem.at[l]) for l in range(levels)]
    for load in loads:
        load.start()
    lane = lax.broadcasted_iota(jnp.int32, (1, LANES), 1)
    tiles = [pack[:1, 2 * half :] for pack in pack_refs]
    for b in range(blocks):
        here = pl.ds(b * count, count)
        a_hi[here, :], a_lo[here, :] = split(unfolded(pack_refs[b][:, :half], members))
        w_hi[here, :], w_lo[here, :] = split(unfolded(pack_refs[b][:, half : 2 * half], members))
    each = LANES // count
    for g in range(0, blocks, each):
        cells = tiles[g]
        for b in range(1, each):
            cells = jnp.where(lane >= b * count, tiles[g + b], cells)
        rho_ref[:, g * count : g * count + LANES] = taper(0, rows, cells, 0) / (members - 1)
    stores = []
    for l in range(levels):
        loads[l].wait()
        high, low = split(state_ref[l])
        covar = product((high, low), (a_hi[...], a_lo[...]), NT) * rho_ref[...]
        total = product(split(covar), (w_hi[...], w_lo[...]), NN)
        out_ref[l] = total[EDGE : rows - EDGE]
        stores.append(pltpu.make_async_copy(out_ref.at[l], out_hbm.at[l, pl.ds(EDGE, rows - 2 * EDGE)], out_sem.at[l]))
        stores[-1].start()
        here = pl.ds(l * EDGE, EDGE)
        for side, part in enumerate((slice(0, EDGE), slice(rows - EDGE, rows))):
            edge_ref[side, here, :] = total[part]
            s_hi[side, here, :] = high[part]
            s_lo[side, here, :] = low[part]
    for store in stores:
        store.wait()


def halo_kernel(blocks, total_hbm, edge_ref, s_hi, s_lo, *refs):
    halo_refs, (out_hbm, out_ref, out_sem) = refs[:blocks], refs[blocks:]
    levels, columns, members = out_hbm.shape
    wide = CAP // SUB * members
    width = halo_refs[0].shape[1] // 2
    starts = (0, columns - EDGE)
    lane = lax.broadcasted_iota(jnp.int32, (1, LANES), 1)
    per = LANES // CAP
    stores = []
    for s, shift in enumerate((-SECT_W, SECT_W)):
        at = s * width
        anom = split(jnp.concatenate([unfolded(h[:, at : at + wide], members) for h in halo_refs], axis=0))
        weight = split(jnp.concatenate([unfolded(h[:, at + wide : at + 2 * wide], members) for h in halo_refs], axis=0))
        tiles = [h[:1, at + 2 * wide : at + width] for h in halo_refs]
        groups = []
        for g in range(0, blocks, per):
            cells = tiles[g]
            for b in range(1, min(per, blocks - g)):
                cells = jnp.where(lane >= b * CAP, tiles[g + b], cells)
            groups.append(cells)
        cells = jnp.concatenate(groups, axis=1)[:, : blocks * CAP]
        rho = taper(starts[s], EDGE, cells, shift) / (members - 1)
        covar = product((s_hi[s], s_lo[s]), anom, NT)
        covar = (covar.reshape(levels, EDGE, -1) * rho[None]).reshape(levels * EDGE, -1)
        out_ref[s] = edge_ref[s] + joined(split(covar), weight, NN)
        for l in range(levels):
            store = pltpu.make_async_copy(
                out_ref.at[s, pl.ds(l * EDGE, EDGE)], out_hbm.at[l, pl.ds(starts[s], EDGE)], out_sem.at[s, l]
            )
            store.start()
            stores.append(store)
    for store in stores:
        store.wait()


def on_device(state_anom, obs_anom, obs_weight, obs_cell, sector_of):
    f32 = jnp.float32
    regions, owners = lax.axis_size("region"), lax.axis_size("state")
    levels, columns, members = state_anom.shape[1:]
    count = obs_anom.shape[1]
    blocks = owners

    slot = jax.ShapeDtypeStruct((SUB, 2 * (CAP // SUB) * members + LANES), f32)
    own_pack, sides, *slots = pl.pallas_call(
        pack_kernel,
        out_shape=[jax.ShapeDtypeStruct((SUB, 2 * (count // SUB) * members + LANES), f32)]
        + [jax.ShapeDtypeStruct((2, SUB, LANES), jnp.int32)]
        + [slot] * (regions - 1),
        in_specs=[HBM] * 4,
        out_specs=[VMEM] * (regions + 1),
        scratch_shapes=[
            pltpu.SMEM((regions,), jnp.int32),
            pltpu.VMEM((count, members), f32),
            pltpu.VMEM((count, members), f32),
            pltpu.VMEM((1, count), jnp.int32),
            pltpu.SemaphoreType.DMA((4,)),
        ],
        compiler_params=limit(8),
        name="pack",
    )(*in_hbm(sector_of, obs_anom, obs_weight, obs_cell))
    got = [exchange(slots[k - 1], "region", k) for k in range(1, regions)]
    packs = [own_pack] + [exchange(own_pack, "state", k) for k in range(1, owners)]
    halo = pl.pallas_call(
        pick_kernel,
        out_shape=jax.ShapeDtypeStruct((SUB, 2 * slot.shape[1]), f32),
        in_specs=[VMEM] * regions,
        out_specs=VMEM,
        compiler_params=limit(4),
        name="pick",
    )(sides, *got)
    halos = [halo] + [exchange(halo, "state", k) for k in range(1, owners)]

    obs = blocks * count
    state = state_anom[0]
    bf16 = jnp.bfloat16
    middle = columns - 2 * EDGE
    edges = (2, levels * EDGE, members)
    total, *kept = pl.pallas_call(
        functools.partial(own_kernel, blocks),
        out_shape=[jax.ShapeDtypeStruct(state.shape, f32), jax.ShapeDtypeStruct(edges, f32)]
        + [jax.ShapeDtypeStruct(edges, bf16)] * 2,
        in_specs=[HBM] + [VMEM] * blocks,
        out_specs=[HBM] + [VMEM] * 3,
        scratch_shapes=[pltpu.VMEM(state.shape, f32), pltpu.VMEM((levels, middle, members), f32)]
        + [pltpu.VMEM((obs, members), bf16)] * 4
        + [pltpu.VMEM((columns, obs), f32)]
        + [pltpu.SemaphoreType.DMA((levels,))] * 2,
        cost_estimate=pl.CostEstimate(
            flops=12 * levels * columns * obs * members, bytes_accessed=8 * state.size + 8 * obs * members, transcendentals=0
        ),
        compiler_params=limit(24),
        name="own",
    )(*in_hbm(state), *packs)
    out = pl.pallas_call(
        functools.partial(halo_kernel, blocks),
        out_shape=jax.ShapeDtypeStruct(state.shape, f32),
        in_specs=[HBM] + [VMEM] * (3 + blocks),
        out_specs=HBM,
        scratch_shapes=[pltpu.VMEM(edges, f32), pltpu.SemaphoreType.DMA((2, levels))],
        input_output_aliases={0: 0},
        compiler_params=limit(16),
        name="halo",
    )(total, *kept, *halos)
    return out[None]


def solution(mesh):
    in_specs = (
        P("region", "state", None, None),
        P("region", "state", None),
        P("region", "state", None),
        P("region", "state"),
        P(),
    )
    out_specs = P("region", "state", None, None)
    return jax.shard_map(on_device, mesh=mesh, in_specs=in_specs, out_specs=out_specs, check_vma=False)
```

```python
import functools

import jax
import jax.numpy as jnp
from jax import lax
from jax.experimental import pallas as pl
from jax.experimental.pallas import tpu as pltpu
from jax.sharding import PartitionSpec as P


SECT_W = 32
LAT = 8
HALF = 4
CAP = 16
EDGE = 2 * HALF * LAT
SUB = 8
LANES = 128
VMEM = pl.BlockSpec(memory_space=pltpu.VMEM)
SMEM = pl.BlockSpec(memory_space=pltpu.SMEM)
HBM = pl.BlockSpec(memory_space=pltpu.HBM)


def limit(mib):
    return pltpu.CompilerParams(vmem_limit_bytes=mib << 20)


def in_hbm(*values):
    return [pltpu.with_memory_space_constraint(value, pltpu.HBM) for value in values]


def partner(index, step, size):
    return index ^ step if size & (size - 1) == 0 else (index + size - step) % size


def target(index, step, size):
    return index ^ step if size & (size - 1) == 0 else (index + step) % size


def exchange(value, axis, step):
    size = lax.axis_size(axis)
    return lax.ppermute(value, axis, [(i, target(i, step, size)) for i in range(size)])


def gaspari(scaled):
    inside = scaled * scaled * (scaled * (scaled * (0.5 - 0.25 * scaled) + 0.625) - 5.0 / 3.0) + 1.0
    floored = jnp.maximum(scaled, 1.0)
    outside = (
        scaled * (scaled * (scaled * (scaled * (scaled / 12.0 - 0.5) + 0.625) + 5.0 / 3.0) - 5.0)
        + 4.0
        - 2.0 / (3.0 * floored)
    )
    return jnp.where(scaled <= 1.0, inside, jnp.where(scaled < 2.0, outside, 0.0))


def taper(first_col, rows, cells, lon_shift):
    cols = first_col + lax.broadcasted_iota(jnp.int32, (rows, cells.shape[1]), 0)
    obs = cells.astype(jnp.int32)
    lon_gap = cols // LAT - (obs // LAT + lon_shift)
    lat_gap = cols % LAT - obs % LAT
    scaled = jnp.sqrt((lon_gap * lon_gap + lat_gap * lat_gap).astype(jnp.float32)) / HALF
    return gaspari(scaled)


def split(value):
    high = value.astype(jnp.bfloat16)
    return high, (value - high.astype(jnp.float32)).astype(jnp.bfloat16)


def product(left, right, dims):
    dot = functools.partial(lax.dot_general, dimension_numbers=(dims, ((), ())), preferred_element_type=jnp.float32)
    return dot(left[0], right[0]) + (dot(left[0], right[1]) + dot(left[1], right[0]))


NT = ((1,), (1,))
NN = ((1,), (0,))


def folded(rows):
    return jnp.concatenate([rows[i : i + SUB] for i in range(0, rows.shape[0], SUB)], axis=1)


def unfolded(tiles, members):
    return jnp.concatenate([tiles[:, i : i + members] for i in range(0, tiles.shape[1], members)], axis=0)


def pack_kernel(sector_hbm, anom_hbm, weight_hbm, cell_hbm, own_ref, *refs):
    side_ref, *slot_refs, sector_ref, anom_ref, weight_ref, cell_ref, sems = refs
    count, members = weight_ref.shape
    loads = [
        pltpu.make_async_copy(cell_hbm, cell_ref, sems.at[0]),
        pltpu.make_async_copy(sector_hbm, sector_ref, sems.at[1]),
        pltpu.make_async_copy(weight_hbm.at[0], weight_ref, sems.at[2]),
        pltpu.make_async_copy(anom_hbm.at[0], anom_ref, sems.at[3]),
    ]
    for load in loads:
        load.start()
    regions = lax.axis_size("region")
    me = lax.axis_index("region")
    entry = lax.broadcasted_iota(jnp.int32, (count, LANES), 0)
    lane = lax.broadcasted_iota(jnp.int32, (count, LANES), 1)
    picks = [
        jnp.where(entry == start + lane % width, 1.0, 0.0).astype(jnp.bfloat16)
        for start, width in ((0, count), (0, CAP), (count - CAP, CAP))
    ]
    loads[0].wait()
    cells = jnp.broadcast_to(cell_ref[...].astype(jnp.float32), (SUB, count)).astype(jnp.bfloat16)
    spread = [lax.dot_general(cells, pick, (NN, ((), ())), preferred_element_type=jnp.float32) for pick in picks]
    loads[1].wait()
    mine = sector_ref[me]
    to_right, from_left, from_right = [], jnp.int32(0), jnp.int32(0)
    for step in range(1, regions):
        to_right.append(sector_ref[target(me, step, regions)] == lax.rem(mine + 1, regions))
        sector = sector_ref[partner(me, step, regions)]
        from_left = jnp.where(sector == lax.rem(mine + regions - 1, regions), step, from_left)
        from_right = jnp.where(sector == lax.rem(mine + 1, regions), step, from_right)
    side_ref[0] = jnp.broadcast_to(from_left, (SUB, LANES))
    side_ref[1] = jnp.broadcast_to(from_right, (SUB, LANES))
    for load in loads[2:]:
        load.wait()
    half = count // SUB * members
    own_ref[:, :half] = folded(anom_ref[...])
    own_ref[:, half : 2 * half] = folded(weight_ref[...])
    own_ref[:, 2 * half :] = spread[0]
    low = (folded(anom_ref[:CAP, :]), folded(weight_ref[:CAP, :]), spread[1])
    high = (folded(anom_ref[count - CAP :, :]), folded(weight_ref[count - CAP :, :]), spread[2])
    wide = CAP // SUB * members
    for slot, up in zip(slot_refs, to_right):
        for (start, stop), lo, hi in zip(((0, wide), (wide, 2 * wide), (2 * wide, 2 * wide + LANES)), low, high):
            slot[:, start:stop] = jnp.where(up, hi, lo)


def pick_kernel(side_ref, *refs):
    *slot_refs, halo_ref = refs
    width = slot_refs[0].shape[1]
    for side in range(2):
        step_of = side_ref[side]
        for at in range(0, width, LANES):
            value = slot_refs[0][:, at : at + LANES]
            for step, slot in enumerate(slot_refs[1:], start=2):
                value = jnp.where(step_of == step, slot[:, at : at + LANES], value)
            halo_ref[:, side * width + at : side * width + at + LANES] = value


def joined(left, right, dims):
    axis = dims[1][0]
    lefts = jnp.concatenate([left[0], left[0], left[1]], axis=1)
    rights = jnp.concatenate([right[0], right[1], right[0]], axis=axis)
    return lax.dot_general(lefts, rights, (dims, ((), ())), preferred_element_type=jnp.float32)


def prep_kernel(state_hbm, hi_ref, lo_ref, state_ref, sems):
    levels, rows = state_ref.shape[:2]
    loads = [pltpu.make_async_copy(state_hbm.at[l], state_ref.at[l], sems.at[l]) for l in range(levels)]
    for load in loads:
        load.start()
    for l in range(levels):
        loads[l].wait()
        here = pl.ds(l * rows, rows)
        hi_ref[here, :], lo_ref[here, :] = split(state_ref[l])


def own_kernel(blocks, s_hi, s_lo, *refs):
    pack_refs, (out_hbm, edge_ref, out_ref, a_hi, a_lo, w_hi, w_lo, out_sem) = refs[:blocks], refs[blocks:]
    levels, middle, members = out_ref.shape
    rows = middle + 2 * EDGE
    half = pack_refs[0].shape[1] // 2 // LANES * LANES
    count = half // members * SUB
    lane = lax.broadcasted_iota(jnp.int32, (1, LANES), 1)
    for b in range(blocks):
        here = pl.ds(b * count, count)
        a_hi[here, :], a_lo[here, :] = split(unfolded(pack_refs[b][:, :half], members))
    for b in range(blocks):
        here = pl.ds(b * count, count)
        w_hi[here, :], w_lo[here, :] = split(unfolded(pack_refs[b][:, half : 2 * half], members))
    each = LANES // count
    groups = []
    for g in range(0, blocks, each):
        cells = pack_refs[g][:1, 2 * half :]
        for b in range(1, each):
            cells = jnp.where(lane >= b * count, pack_refs[g + b][:1, 2 * half :], cells)
        groups.append(taper(0, rows, cells, 0) / (members - 1))
    rho = jnp.concatenate(groups, axis=1)
    stores = []
    for l in range(levels):
        here = pl.ds(l * rows, rows)
        covar = product((s_hi[here, :], s_lo[here, :]), (a_hi[...], a_lo[...]), NT) * rho
        total = product(split(covar), (w_hi[...], w_lo[...]), NN)
        out_ref[l] = total[EDGE : rows - EDGE]
        stores.append(pltpu.make_async_copy(out_ref.at[l], out_hbm.at[l, pl.ds(EDGE, middle)], out_sem.at[l]))
        stores[-1].start()
        for side, part in enumerate((slice(0, EDGE), slice(rows - EDGE, rows))):
            edge_ref[side, pl.ds(l * EDGE, EDGE), :] = total[part]
    for store in stores:
        store.wait()


def halo_kernel(blocks, total_hbm, edge_ref, s_hi, s_lo, *refs):
    halo_refs, (out_hbm, out_ref, out_sem) = refs[:blocks], refs[blocks:]
    levels, columns, members = out_hbm.shape
    wide = CAP // SUB * members
    width = halo_refs[0].shape[1] // 2
    starts = (0, columns - EDGE)
    lane = lax.broadcasted_iota(jnp.int32, (1, LANES), 1)
    per = LANES // CAP
    stores = []
    for s, shift in enumerate((-SECT_W, SECT_W)):
        at = s * width
        anom = split(jnp.concatenate([unfolded(h[:, at : at + wide], members) for h in halo_refs], axis=0))
        weight = split(jnp.concatenate([unfolded(h[:, at + wide : at + 2 * wide], members) for h in halo_refs], axis=0))
        tiles = [h[:1, at + 2 * wide : at + width] for h in halo_refs]
        groups = []
        for g in range(0, blocks, per):
            cells = tiles[g]
            for b in range(1, min(per, blocks - g)):
                cells = jnp.where(lane >= b * CAP, tiles[g + b], cells)
            groups.append(cells)
        cells = jnp.concatenate(groups, axis=1)[:, : blocks * CAP]
        rho = taper(starts[s], EDGE, cells, shift) / (members - 1)
        high, low = (
            jnp.concatenate([ref[l * columns + starts[s] : l * columns + starts[s] + EDGE, :] for l in range(levels)], axis=0)
            for ref in (s_hi, s_lo)
        )
        both = jnp.concatenate(anom, axis=0)
        dot = functools.partial(lax.dot_general, dimension_numbers=(NT, ((), ())), preferred_element_type=jnp.float32)
        wide_dot = dot(high, both)
        count = blocks * CAP
        covar = wide_dot[:, :count] + (wide_dot[:, count:] + dot(low, anom[0]))
        covar = (covar.reshape(levels, EDGE, -1) * rho[None]).reshape(levels * EDGE, -1)
        out_ref[s] = edge_ref[s] + joined(split(covar), weight, NN)
        for l in range(levels):
            store = pltpu.make_async_copy(
                out_ref.at[s, pl.ds(l * EDGE, EDGE)], out_hbm.at[l, pl.ds(starts[s], EDGE)], out_sem.at[s, l]
            )
            store.start()
            stores.append(store)
    for store in stores:
        store.wait()


def on_device(state_anom, obs_anom, obs_weight, obs_cell, sector_of):
    f32 = jnp.float32
    regions, owners = lax.axis_size("region"), lax.axis_size("state")
    levels, columns, members = state_anom.shape[1:]
    count = obs_anom.shape[1]
    blocks = owners

    slot = jax.ShapeDtypeStruct((SUB, 2 * (CAP // SUB) * members + LANES), f32)
    own_pack, sides, *slots = pl.pallas_call(
        pack_kernel,
        out_shape=[jax.ShapeDtypeStruct((SUB, 2 * (count // SUB) * members + LANES), f32)]
        + [jax.ShapeDtypeStruct((2, SUB, LANES), jnp.int32)]
        + [slot] * (regions - 1),
        in_specs=[HBM] * 4,
        out_specs=[VMEM] * (regions + 1),
        scratch_shapes=[
            pltpu.SMEM((regions,), jnp.int32),
            pltpu.VMEM((count, members), f32),
            pltpu.VMEM((count, members), f32),
            pltpu.VMEM((1, count), jnp.int32),
            pltpu.SemaphoreType.DMA((4,)),
        ],
        compiler_params=limit(8),
        name="pack",
    )(*in_hbm(sector_of, obs_anom, obs_weight, obs_cell))
    got = [exchange(slots[k - 1], "region", k) for k in range(1, regions)]
    packs = [own_pack] + [exchange(own_pack, "state", k) for k in range(1, owners)]
    halo = pl.pallas_call(
        pick_kernel,
        out_shape=jax.ShapeDtypeStruct((SUB, 2 * slot.shape[1]), f32),
        in_specs=[VMEM] * regions,
        out_specs=VMEM,
        compiler_params=limit(4),
        name="pick",
    )(sides, *got)
    halos = [halo] + [exchange(halo, "state", k) for k in range(1, owners)]

    obs = blocks * count
    state = state_anom[0]
    bf16 = jnp.bfloat16
    middle = columns - 2 * EDGE
    edges = (2, levels * EDGE, members)
    halves = (levels * columns, members)
    s_hi, s_lo = pl.pallas_call(
        prep_kernel,
        out_shape=[jax.ShapeDtypeStruct(halves, bf16)] * 2,
        in_specs=[HBM],
        out_specs=[VMEM] * 2,
        scratch_shapes=[pltpu.VMEM(state.shape, f32), pltpu.SemaphoreType.DMA((levels,))],
        compiler_params=limit(8),
        name="prep",
    )(*in_hbm(state))
    total, edge = pl.pallas_call(
        functools.partial(own_kernel, blocks),
        out_shape=[jax.ShapeDtypeStruct(state.shape, f32), jax.ShapeDtypeStruct(edges, f32)],
        in_specs=[VMEM] * (2 + blocks),
        out_specs=[HBM, VMEM],
        scratch_shapes=[pltpu.VMEM((levels, middle, members), f32)]
        + [pltpu.VMEM((obs, members), bf16)] * 4
        + [pltpu.SemaphoreType.DMA((levels,))],
        cost_estimate=pl.CostEstimate(
            flops=12 * levels * columns * obs * members, bytes_accessed=8 * state.size + 8 * obs * members, transcendentals=0
        ),
        compiler_params=limit(24),
        name="own",
    )(s_hi, s_lo, *packs)
    out = pl.pallas_call(
        functools.partial(halo_kernel, blocks),
        out_shape=jax.ShapeDtypeStruct(state.shape, f32),
        in_specs=[HBM] + [VMEM] * (3 + blocks),
        out_specs=HBM,
        scratch_shapes=[pltpu.VMEM(edges, f32), pltpu.SemaphoreType.DMA((2, levels))],
        input_output_aliases={0: 0},
        compiler_params=limit(16),
        name="halo",
    )(total, edge, s_hi, s_lo, *halos)
    return out[None]


def solution(mesh):
    in_specs = (
        P("region", "state", None, None),
        P("region", "state", None),
        P("region", "state", None),
        P("region", "state"),
        P(),
    )
    out_specs = P("region", "state", None, None)
    return jax.shard_map(on_device, mesh=mesh, in_specs=in_specs, out_specs=out_specs, check_vma=False)
```

```python
import functools

import jax
import jax.numpy as jnp
from jax import lax
from jax.experimental import pallas as pl
from jax.experimental.pallas import tpu as pltpu
from jax.sharding import PartitionSpec as P


SECT_W = 32
LAT = 8
HALF = 4
CAP = 16
EDGE = 2 * HALF * LAT
SUB = 8
LANES = 128
VMEM = pl.BlockSpec(memory_space=pltpu.VMEM)
SMEM = pl.BlockSpec(memory_space=pltpu.SMEM)
HBM = pl.BlockSpec(memory_space=pltpu.HBM)


def limit(mib):
    return pltpu.CompilerParams(vmem_limit_bytes=mib << 20)


def in_hbm(*values):
    return [pltpu.with_memory_space_constraint(value, pltpu.HBM) for value in values]


def target(index, step, size):
    return index ^ step if size & (size - 1) == 0 else (index + step) % size


def exchange(value, axis, step):
    size = lax.axis_size(axis)
    return lax.ppermute(value, axis, [(i, target(i, step, size)) for i in range(size)])


def gaspari(scaled):
    inside = scaled * scaled * (scaled * (scaled * (0.5 - 0.25 * scaled) + 0.625) - 5.0 / 3.0) + 1.0
    floored = jnp.maximum(scaled, 1.0)
    outside = (
        scaled * (scaled * (scaled * (scaled * (scaled / 12.0 - 0.5) + 0.625) + 5.0 / 3.0) - 5.0)
        + 4.0
        - 2.0 / (3.0 * floored)
    )
    return jnp.where(scaled <= 1.0, inside, jnp.where(scaled < 2.0, outside, 0.0))


def taper(first_col, rows, cells, lon_shift):
    cols = first_col + lax.broadcasted_iota(jnp.int32, (rows, cells.shape[1]), 0)
    obs = cells.astype(jnp.int32)
    lon_gap = cols // LAT - (obs // LAT + lon_shift)
    lat_gap = cols % LAT - obs % LAT
    scaled = jnp.sqrt((lon_gap * lon_gap + lat_gap * lat_gap).astype(jnp.float32)) / HALF
    return gaspari(scaled)


def split(value):
    high = value.astype(jnp.bfloat16)
    return high, (value - high.astype(jnp.float32)).astype(jnp.bfloat16)


def product(left, right, dims):
    dot = functools.partial(lax.dot_general, dimension_numbers=(dims, ((), ())), preferred_element_type=jnp.float32)
    return dot(left[0], right[0]) + (dot(left[0], right[1]) + dot(left[1], right[0]))


NT = ((1,), (1,))
NN = ((1,), (0,))


def folded(rows):
    return jnp.concatenate([rows[i : i + SUB] for i in range(0, rows.shape[0], SUB)], axis=1)


def unfolded(tiles, members):
    return jnp.concatenate([tiles[:, i : i + members] for i in range(0, tiles.shape[1], members)], axis=0)


def pack_kernel(sector_hbm, anom_hbm, weight_hbm, cell_hbm, own_ref, *refs):
    side_ref, cross_ref, *near_refs, sector_ref, anom_ref, weight_ref, cell_ref, sems = refs
    count, members = weight_ref.shape
    loads = [
        pltpu.make_async_copy(cell_hbm, cell_ref, sems.at[0]),
        pltpu.make_async_copy(sector_hbm, sector_ref, sems.at[1]),
        pltpu.make_async_copy(weight_hbm.at[0], weight_ref, sems.at[2]),
        pltpu.make_async_copy(anom_hbm.at[0], anom_ref, sems.at[3]),
    ]
    for load in loads:
        load.start()
    regions = lax.axis_size("region")
    half_way = regions // 2
    me = lax.axis_index("region")
    entry = lax.broadcasted_iota(jnp.int32, (count, LANES), 0)
    lane = lax.broadcasted_iota(jnp.int32, (count, LANES), 1)
    picks = [
        jnp.where(entry == start + lane % width, 1.0, 0.0).astype(jnp.bfloat16)
        for start, width in ((0, count), (0, CAP), (count - CAP, CAP))
    ]
    loads[0].wait()
    cells = jnp.broadcast_to(cell_ref[...].astype(jnp.float32), (SUB, count)).astype(jnp.bfloat16)
    spread = [lax.dot_general(cells, pick, (NN, ((), ())), preferred_element_type=jnp.float32) for pick in picks]
    loads[1].wait()
    mine = sector_ref[me]
    far = me ^ half_way
    is_next = lambda first, second: second == lax.rem(first + 1, regions)
    from_left, from_right, to_right = jnp.int32(0), jnp.int32(0), []
    for step in range(1, regions):
        sector = sector_ref[me ^ step]
        from_left = jnp.where(is_next(sector, mine), step, from_left)
        from_right = jnp.where(is_next(mine, sector), step, from_right)
    codes = [from_left, from_right]
    for step in range(1, half_way):
        sector = sector_ref[me ^ step]
        to_right.append(is_next(mine, sector))
        codes.append(is_next(sector_ref[far], sector).astype(jnp.int32))
    for i, code in enumerate(codes):
        side_ref[i] = jnp.broadcast_to(code, (SUB, LANES))
    for load in loads[2:]:
        load.wait()
    half = count // SUB * members
    own_ref[:, :half] = folded(anom_ref[...])
    own_ref[:, half : 2 * half] = folded(weight_ref[...])
    own_ref[:, 2 * half :] = spread[0]
    low = (folded(anom_ref[:CAP, :]), folded(weight_ref[:CAP, :]), spread[1])
    high = (folded(anom_ref[count - CAP :, :]), folded(weight_ref[count - CAP :, :]), spread[2])
    wide = CAP // SUB * members
    width = 2 * wide + LANES
    for (start, stop), lo, hi in zip(((0, wide), (wide, 2 * wide), (2 * wide, width)), low, high):
        cross_ref[:, start:stop] = lo
        cross_ref[:, width + start : width + stop] = hi
        for near, up in zip(near_refs, to_right):
            near[:, start:stop] = jnp.where(up, hi, lo)


def relay_kernel(side_ref, cross_ref, *pass_refs):
    width = pass_refs[0].shape[1]
    for step, out in enumerate(pass_refs, start=1):
        up = side_ref[1 + step] == 1
        for at in range(0, width, LANES):
            out[:, at : at + LANES] = jnp.where(up, cross_ref[:, width + at : width + at + LANES], cross_ref[:, at : at + LANES])


def pick_kernel(side_ref, cross_ref, *refs):
    *slot_refs, halo_ref = refs
    width = slot_refs[0].shape[1]
    half_way = len(slot_refs) // 2 + 1
    near, passed = slot_refs[: half_way - 1], slot_refs[half_way - 1 :]
    for side in range(2):
        code = side_ref[side]
        for at in range(0, width, LANES):
            here = (1 - side) * width + at
            value = cross_ref[:, here : here + LANES]
            for step in range(1, half_way):
                value = jnp.where(code == step, near[step - 1][:, at : at + LANES], value)
                value = jnp.where(code == step + half_way, passed[step - 1][:, at : at + LANES], value)
            halo_ref[:, side * width + at : side * width + at + LANES] = value


def joined(left, right, dims):
    axis = dims[1][0]
    lefts = jnp.concatenate([left[0], left[0], left[1]], axis=1)
    rights = jnp.concatenate([right[0], right[1], right[0]], axis=axis)
    return lax.dot_general(lefts, rights, (dims, ((), ())), preferred_element_type=jnp.float32)


def prep_kernel(state_hbm, hi_ref, lo_ref, state_ref, sems):
    levels, rows = state_ref.shape[:2]
    loads = [pltpu.make_async_copy(state_hbm.at[l], state_ref.at[l], sems.at[l]) for l in range(levels)]
    for load in loads:
        load.start()
    for l in range(levels):
        loads[l].wait()
        here = pl.ds(l * rows, rows)
        hi_ref[here, :], lo_ref[here, :] = split(state_ref[l])


def own_kernel(blocks, s_hi, s_lo, *refs):
    pack_refs, (out_hbm, edge_ref, out_ref, a_hi, a_lo, w_hi, w_lo, out_sem) = refs[:blocks], refs[blocks:]
    levels, middle, members = out_ref.shape
    rows = middle + 2 * EDGE
    half = pack_refs[0].shape[1] // 2 // LANES * LANES
    count = half // members * SUB
    lane = lax.broadcasted_iota(jnp.int32, (1, LANES), 1)
    for b in range(blocks):
        here = pl.ds(b * count, count)
        a_hi[here, :], a_lo[here, :] = split(unfolded(pack_refs[b][:, :half], members))
    for b in range(blocks):
        here = pl.ds(b * count, count)
        w_hi[here, :], w_lo[here, :] = split(unfolded(pack_refs[b][:, half : 2 * half], members))
    each = LANES // count
    groups = []
    for g in range(0, blocks, each):
        cells = pack_refs[g][:1, 2 * half :]
        for b in range(1, each):
            cells = jnp.where(lane >= b * count, pack_refs[g + b][:1, 2 * half :], cells)
        groups.append(taper(0, rows, cells, 0) / (members - 1))
    rho = jnp.concatenate(groups, axis=1)
    stores = []
    for l in range(levels):
        here = pl.ds(l * rows, rows)
        covar = product((s_hi[here, :], s_lo[here, :]), (a_hi[...], a_lo[...]), NT) * rho
        total = product(split(covar), (w_hi[...], w_lo[...]), NN)
        out_ref[l] = total[EDGE : rows - EDGE]
        stores.append(pltpu.make_async_copy(out_ref.at[l], out_hbm.at[l, pl.ds(EDGE, middle)], out_sem.at[l]))
        stores[-1].start()
        for side, part in enumerate((slice(0, EDGE), slice(rows - EDGE, rows))):
            edge_ref[side, pl.ds(l * EDGE, EDGE), :] = total[part]
    for store in stores:
        store.wait()


def halo_kernel(blocks, total_hbm, edge_ref, s_hi, s_lo, *refs):
    halo_refs, (out_hbm, out_ref, out_sem) = refs[:blocks], refs[blocks:]
    levels, columns, members = out_hbm.shape
    wide = CAP // SUB * members
    width = halo_refs[0].shape[1] // 2
    starts = (0, columns - EDGE)
    lane = lax.broadcasted_iota(jnp.int32, (1, LANES), 1)
    per = LANES // CAP
    stores = []
    for s, shift in enumerate((-SECT_W, SECT_W)):
        at = s * width
        anom = split(jnp.concatenate([unfolded(h[:, at : at + wide], members) for h in halo_refs], axis=0))
        weight = split(jnp.concatenate([unfolded(h[:, at + wide : at + 2 * wide], members) for h in halo_refs], axis=0))
        tiles = [h[:1, at + 2 * wide : at + width] for h in halo_refs]
        groups = []
        for g in range(0, blocks, per):
            cells = tiles[g]
            for b in range(1, min(per, blocks - g)):
                cells = jnp.where(lane >= b * CAP, tiles[g + b], cells)
            groups.append(cells)
        cells = jnp.concatenate(groups, axis=1)[:, : blocks * CAP]
        rho = taper(starts[s], EDGE, cells, shift) / (members - 1)
        high, low = (
            jnp.concatenate([ref[l * columns + starts[s] : l * columns + starts[s] + EDGE, :] for l in range(levels)], axis=0)
            for ref in (s_hi, s_lo)
        )
        both = jnp.concatenate(anom, axis=0)
        dot = functools.partial(lax.dot_general, dimension_numbers=(NT, ((), ())), preferred_element_type=jnp.float32)
        wide_dot = dot(high, both)
        count = blocks * CAP
        covar = wide_dot[:, :count] + (wide_dot[:, count:] + dot(low, anom[0]))
        covar = (covar.reshape(levels, EDGE, -1) * rho[None]).reshape(levels * EDGE, -1)
        out_ref[s] = edge_ref[s] + joined(split(covar), weight, NN)
        for l in range(levels):
            store = pltpu.make_async_copy(
                out_ref.at[s, pl.ds(l * EDGE, EDGE)], out_hbm.at[l, pl.ds(starts[s], EDGE)], out_sem.at[s, l]
            )
            store.start()
            stores.append(store)
    for store in stores:
        store.wait()


def on_device(state_anom, obs_anom, obs_weight, obs_cell, sector_of):
    f32 = jnp.float32
    regions, owners = lax.axis_size("region"), lax.axis_size("state")
    levels, columns, members = state_anom.shape[1:]
    count = obs_anom.shape[1]
    blocks = owners

    assert regions & (regions - 1) == 0
    half_way = regions // 2
    slot = jax.ShapeDtypeStruct((SUB, 2 * (CAP // SUB) * members + LANES), f32)
    pair = jax.ShapeDtypeStruct((SUB, 2 * slot.shape[1]), f32)
    near = range(1, half_way)
    own_pack, sides, cross, *slots = pl.pallas_call(
        pack_kernel,
        out_shape=[jax.ShapeDtypeStruct((SUB, 2 * (count // SUB) * members + LANES), f32)]
        + [jax.ShapeDtypeStruct((half_way + 1, SUB, LANES), jnp.int32), pair]
        + [slot] * len(near),
        in_specs=[HBM] * 4,
        out_specs=[VMEM] * (3 + len(near)),
        scratch_shapes=[
            pltpu.SMEM((regions,), jnp.int32),
            pltpu.VMEM((count, members), f32),
            pltpu.VMEM((count, members), f32),
            pltpu.VMEM((1, count), jnp.int32),
            pltpu.SemaphoreType.DMA((4,)),
        ],
        compiler_params=limit(8),
        name="pack",
    )(*in_hbm(sector_of, obs_anom, obs_weight, obs_cell))
    crossed = exchange(cross, "region", half_way)
    direct = [exchange(slots[k - 1], "region", k) for k in near]
    relayed = pl.pallas_call(
        relay_kernel,
        out_shape=[slot] * len(near),
        in_specs=[VMEM] * 2,
        out_specs=[VMEM] * len(near),
        compiler_params=limit(4),
        name="relay",
    )(sides, crossed)
    passed = [exchange(relayed[k - 1], "region", k) for k in near]
    packs = [own_pack] + [exchange(own_pack, "state", k) for k in range(1, owners)]
    halo = pl.pallas_call(
        pick_kernel,
        out_shape=pair,
        in_specs=[VMEM] * (2 + 2 * len(near)),
        out_specs=VMEM,
        compiler_params=limit(4),
        name="pick",
    )(sides, crossed, *direct, *passed)
    halos = [halo] + [exchange(halo, "state", k) for k in range(1, owners)]

    obs = blocks * count
    state = state_anom[0]
    bf16 = jnp.bfloat16
    middle = columns - 2 * EDGE
    edges = (2, levels * EDGE, members)
    halves = (levels * columns, members)
    s_hi, s_lo = pl.pallas_call(
        prep_kernel,
        out_shape=[jax.ShapeDtypeStruct(halves, bf16)] * 2,
        in_specs=[HBM],
        out_specs=[VMEM] * 2,
        scratch_shapes=[pltpu.VMEM(state.shape, f32), pltpu.SemaphoreType.DMA((levels,))],
        compiler_params=limit(8),
        name="prep",
    )(*in_hbm(state))
    total, edge = pl.pallas_call(
        functools.partial(own_kernel, blocks),
        out_shape=[jax.ShapeDtypeStruct(state.shape, f32), jax.ShapeDtypeStruct(edges, f32)],
        in_specs=[VMEM] * (2 + blocks),
        out_specs=[HBM, VMEM],
        scratch_shapes=[pltpu.VMEM((levels, middle, members), f32)]
        + [pltpu.VMEM((obs, members), bf16)] * 4
        + [pltpu.SemaphoreType.DMA((levels,))],
        cost_estimate=pl.CostEstimate(
            flops=12 * levels * columns * obs * members, bytes_accessed=8 * state.size + 8 * obs * members, transcendentals=0
        ),
        compiler_params=limit(24),
        name="own",
    )(s_hi, s_lo, *packs)
    out = pl.pallas_call(
        functools.partial(halo_kernel, blocks),
        out_shape=jax.ShapeDtypeStruct(state.shape, f32),
        in_specs=[HBM] + [VMEM] * (3 + blocks),
        out_specs=HBM,
        scratch_shapes=[pltpu.VMEM(edges, f32), pltpu.SemaphoreType.DMA((2, levels))],
        input_output_aliases={0: 0},
        compiler_params=limit(16),
        name="halo",
    )(total, edge, s_hi, s_lo, *halos)
    return out[None]


def solution(mesh):
    in_specs = (
        P("region", "state", None, None),
        P("region", "state", None),
        P("region", "state", None),
        P("region", "state"),
        P(),
    )
    out_specs = P("region", "state", None, None)
    return jax.shard_map(on_device, mesh=mesh, in_specs=in_specs, out_specs=out_specs, check_vma=False)
```

```python
import functools

import jax
import jax.numpy as jnp
from jax import lax
from jax.experimental import pallas as pl
from jax.experimental.pallas import tpu as pltpu
from jax.sharding import PartitionSpec as P


SECT_W = 32
LAT = 8
HALF = 4
CAP = 16
EDGE = 2 * HALF * LAT
SUB = 8
LANES = 128
VMEM = pl.BlockSpec(memory_space=pltpu.VMEM)
SMEM = pl.BlockSpec(memory_space=pltpu.SMEM)
HBM = pl.BlockSpec(memory_space=pltpu.HBM)


def limit(mib):
    return pltpu.CompilerParams(vmem_limit_bytes=mib << 20)


def in_hbm(*values):
    return [pltpu.with_memory_space_constraint(value, pltpu.HBM) for value in values]


def target(index, step, size):
    return index ^ step if size & (size - 1) == 0 else (index + step) % size


def exchange(value, axis, step):
    size = lax.axis_size(axis)
    return lax.ppermute(value, axis, [(i, target(i, step, size)) for i in range(size)])


def gather(value, axis):
    size = lax.axis_size(axis)
    steps = (2, 1) if size == 4 else range(size - 1, 0, -1)
    got = {step: exchange(value, axis, step) for step in steps}
    if size == 4:
        got[3] = [exchange(got[1][0], axis, 2), exchange(got[2][1], axis, 1)]
    return [(half[0], half[1]) if isinstance(half, list) else half for half in [value] + [got[k] for k in range(1, size)]]


def gaspari(scaled):
    inside = scaled * scaled * (scaled * (scaled * (0.5 - 0.25 * scaled) + 0.625) - 5.0 / 3.0) + 1.0
    floored = jnp.maximum(scaled, 1.0)
    outside = (
        scaled * (scaled * (scaled * (scaled * (scaled / 12.0 - 0.5) + 0.625) + 5.0 / 3.0) - 5.0)
        + 4.0
        - 2.0 / (3.0 * floored)
    )
    return jnp.where(scaled <= 1.0, inside, jnp.where(scaled < 2.0, outside, 0.0))


def taper(first_col, rows, cells, lon_shift):
    cols = first_col + lax.broadcasted_iota(jnp.int32, (rows, cells.shape[1]), 0)
    obs = cells.astype(jnp.int32)
    lon_gap = cols // LAT - (obs // LAT + lon_shift)
    lat_gap = cols % LAT - obs % LAT
    scaled = jnp.sqrt((lon_gap * lon_gap + lat_gap * lat_gap).astype(jnp.float32)) / HALF
    return gaspari(scaled)


def split(value):
    high = value.astype(jnp.bfloat16)
    return high, (value - high.astype(jnp.float32)).astype(jnp.bfloat16)


def product(left, right, dims):
    dot = functools.partial(lax.dot_general, dimension_numbers=(dims, ((), ())), preferred_element_type=jnp.float32)
    return dot(left[0], right[0]) + (dot(left[0], right[1]) + dot(left[1], right[0]))


NT = ((1,), (1,))
NN = ((1,), (0,))


def folded(rows):
    return jnp.concatenate([rows[i : i + SUB] for i in range(0, rows.shape[0], SUB)], axis=1)


def unfolded(tiles, members):
    return jnp.concatenate([tiles[:, i : i + members] for i in range(0, tiles.shape[1], members)], axis=0)


def pack_kernel(sector_hbm, anom_hbm, weight_hbm, cell_hbm, own_ref, *refs):
    side_ref, cross_ref, *near_refs, sector_ref, anom_ref, weight_ref, cell_ref, sems = refs
    count, members = weight_ref.shape
    loads = [
        pltpu.make_async_copy(cell_hbm, cell_ref, sems.at[0]),
        pltpu.make_async_copy(sector_hbm, sector_ref, sems.at[1]),
        pltpu.make_async_copy(weight_hbm.at[0], weight_ref, sems.at[2]),
        pltpu.make_async_copy(anom_hbm.at[0], anom_ref, sems.at[3]),
    ]
    for load in loads:
        load.start()
    regions = lax.axis_size("region")
    half_way = regions // 2
    me = lax.axis_index("region")
    entry = lax.broadcasted_iota(jnp.int32, (count, LANES), 0)
    lane = lax.broadcasted_iota(jnp.int32, (count, LANES), 1)
    picks = [
        jnp.where(entry == start + lane % width, 1.0, 0.0).astype(jnp.bfloat16)
        for start, width in ((0, count), (0, CAP), (count - CAP, CAP))
    ]
    loads[0].wait()
    cells = jnp.broadcast_to(cell_ref[...].astype(jnp.float32), (SUB, count)).astype(jnp.bfloat16)
    spread = [lax.dot_general(cells, pick, (NN, ((), ())), preferred_element_type=jnp.float32) for pick in picks]
    loads[1].wait()
    mine = sector_ref[me]
    far = me ^ half_way
    is_next = lambda first, second: second == lax.rem(first + 1, regions)
    from_left, from_right, to_right = jnp.int32(0), jnp.int32(0), []
    for step in range(1, regions):
        sector = sector_ref[me ^ step]
        from_left = jnp.where(is_next(sector, mine), step, from_left)
        from_right = jnp.where(is_next(mine, sector), step, from_right)
    codes = [from_left, from_right]
    for step in range(1, half_way):
        sector = sector_ref[me ^ step]
        to_right.append(is_next(mine, sector))
        codes.append(is_next(sector_ref[far], sector).astype(jnp.int32))
    for i, code in enumerate(codes):
        side_ref[i] = jnp.broadcast_to(code, (SUB, LANES))
    for load in loads[2:]:
        load.wait()
    half = count // SUB * members
    own_ref[0, :, :half] = folded(anom_ref[...])
    own_ref[1, :, :half] = folded(weight_ref[...])
    own_ref[0, :, half:] = spread[0]
    own_ref[1, :, half:] = spread[0]
    low = (folded(anom_ref[:CAP, :]), folded(weight_ref[:CAP, :]), spread[1])
    high = (folded(anom_ref[count - CAP :, :]), folded(weight_ref[count - CAP :, :]), spread[2])
    wide = CAP // SUB * members
    upper = lax.broadcasted_iota(jnp.int32, (SUB, LANES), 0) >= SUB // 2
    for i, (start, stop) in enumerate(((0, wide), (wide, 2 * wide), (2 * wide, 2 * wide + LANES))):
        if i < 2:
            cross_ref[:, start:stop] = low[i]
            cross_ref[:, 2 * wide + start : 2 * wide + stop] = high[i]
        for near, up in zip(near_refs, to_right):
            near[:, start:stop] = jnp.where(up, high[i], low[i])
    cross_ref[:, 4 * wide :] = jnp.where(upper, high[2], low[2])


def pair_tile(pair_ref, upper, at, width):
    if at < width - LANES:
        at += upper * (width - LANES)
        return pair_ref[:, at : at + LANES]
    row = upper * (SUB // 2)
    return jnp.broadcast_to(pair_ref[row : row + 1, pair_ref.shape[1] - LANES :], (SUB, LANES))


def relay_kernel(side_ref, cross_ref, *pass_refs):
    width = pass_refs[0].shape[1]
    for step, out in enumerate(pass_refs, start=1):
        up = side_ref[1 + step] == 1
        for at in range(0, width, LANES):
            out[:, at : at + LANES] = jnp.where(up, pair_tile(cross_ref, 1, at, width), pair_tile(cross_ref, 0, at, width))


def pick_kernel(side_ref, cross_ref, *refs):
    *slot_refs, halo_ref = refs
    width = slot_refs[0].shape[1]
    half_way = len(slot_refs) // 2 + 1
    near, passed = slot_refs[: half_way - 1], slot_refs[half_way - 1 :]
    upper = lax.broadcasted_iota(jnp.int32, (SUB, LANES), 0) >= SUB // 2
    for at in range(0, width, LANES):
        values = []
        for side in range(2):
            code = side_ref[side]
            value = pair_tile(cross_ref, 1 - side, at, width)
            for step in range(1, half_way):
                value = jnp.where(code == step, near[step - 1][:, at : at + LANES], value)
                value = jnp.where(code == step + half_way, passed[step - 1][:, at : at + LANES], value)
            values.append(value)
        if at < width - LANES:
            for side, value in enumerate(values):
                start = side * (width - LANES) + at
                halo_ref[:, start : start + LANES] = value
        else:
            halo_ref[:, 2 * at :] = jnp.where(upper, values[1], values[0])


def joined(left, right, dims):
    axis = dims[1][0]
    lefts = jnp.concatenate([left[0], left[0], left[1]], axis=1)
    rights = jnp.concatenate([right[0], right[1], right[0]], axis=axis)
    return lax.dot_general(lefts, rights, (dims, ((), ())), preferred_element_type=jnp.float32)


def prep_kernel(state_hbm, hi_ref, lo_ref, state_ref, sems):
    levels, rows = state_ref.shape[:2]
    loads = [pltpu.make_async_copy(state_hbm.at[l], state_ref.at[l], sems.at[l]) for l in range(levels)]
    for load in loads:
        load.start()
    for l in range(levels):
        loads[l].wait()
        here = pl.ds(l * rows, rows)
        hi_ref[here, :], lo_ref[here, :] = split(state_ref[l])


def own_kernel(tree, s_hi, s_lo, *refs):
    *flat, out_hbm, edge_ref, out_ref, a_hi, a_lo, w_hi, w_lo, out_sem = refs
    packs = [pack if isinstance(pack, tuple) else (pack.at[0], pack.at[1]) for pack in jax.tree.unflatten(tree, flat)]
    blocks = len(packs)
    levels, middle, members = out_ref.shape
    rows = middle + 2 * EDGE
    half = packs[0][0].shape[1] - LANES
    count = half // members * SUB
    lane = lax.broadcasted_iota(jnp.int32, (1, LANES), 1)
    for b in range(blocks):
        here = pl.ds(b * count, count)
        a_hi[here, :], a_lo[here, :] = split(unfolded(packs[b][0][:, :half], members))
    for b in range(blocks):
        here = pl.ds(b * count, count)
        w_hi[here, :], w_lo[here, :] = split(unfolded(packs[b][1][:, :half], members))
    each = LANES // count
    groups = []
    for g in range(0, blocks, each):
        cells = packs[g][0][:1, half:]
        for b in range(1, each):
            cells = jnp.where(lane >= b * count, packs[g + b][0][:1, half:], cells)
        groups.append(taper(0, rows, cells, 0) / (members - 1))
    rho = jnp.concatenate(groups, axis=1)
    stores = []
    for l in range(levels):
        here = pl.ds(l * rows, rows)
        covar = product((s_hi[here, :], s_lo[here, :]), (a_hi[...], a_lo[...]), NT) * rho
        total = product(split(covar), (w_hi[...], w_lo[...]), NN)
        out_ref[l] = total[EDGE : rows - EDGE]
        stores.append(pltpu.make_async_copy(out_ref.at[l], out_hbm.at[l, pl.ds(EDGE, middle)], out_sem.at[l]))
        stores[-1].start()
        for side, part in enumerate((slice(0, EDGE), slice(rows - EDGE, rows))):
            edge_ref[side, pl.ds(l * EDGE, EDGE), :] = total[part]
    for store in stores:
        store.wait()


def halo_kernel(blocks, total_hbm, edge_ref, s_hi, s_lo, *refs):
    halo_refs, (out_hbm, out_ref, out_sem) = refs[:blocks], refs[blocks:]
    levels, columns, members = out_hbm.shape
    wide = CAP // SUB * members
    count = blocks * CAP
    starts = (0, columns - EDGE)
    lane = lax.broadcasted_iota(jnp.int32, (1, LANES), 1)
    per = LANES // CAP
    dot = functools.partial(lax.dot_general, dimension_numbers=(NT, ((), ())), preferred_element_type=jnp.float32)
    covars, weights = [], []
    for s, shift in enumerate((-SECT_W, SECT_W)):
        at = 2 * s * wide
        anom = split(jnp.concatenate([unfolded(h[:, at : at + wide], members) for h in halo_refs], axis=0))
        both = jnp.concatenate(anom, axis=0)
        high, low = (
            jnp.concatenate([ref[l * columns + starts[s] : l * columns + starts[s] + EDGE, :] for l in range(levels)], axis=0)
            for ref in (s_hi, s_lo)
        )
        wide_dot = dot(high, both)
        covar = wide_dot[:, :count] + (wide_dot[:, count:] + dot(low, anom[0]))
        row = s * (SUB // 2)
        tiles = [h[row : row + 1, 4 * wide :] for h in halo_refs]
        groups = []
        for g in range(0, blocks, per):
            cells = tiles[g]
            for b in range(1, min(per, blocks - g)):
                cells = jnp.where(lane >= b * CAP, tiles[g + b], cells)
            groups.append(cells)
        cells = jnp.concatenate(groups, axis=1)[:, :count]
        rho = taper(starts[s], EDGE, cells, shift) / (members - 1)
        covars.append(split((covar.reshape(levels, EDGE, -1) * rho[None]).reshape(levels * EDGE, -1)))
        weights.append(split(jnp.concatenate([unfolded(h[:, at + wide : at + 2 * wide], members) for h in halo_refs], axis=0)))
    stores = []
    for s in range(2):
        out_ref[s] = edge_ref[s] + joined(covars[s], weights[s], NN)
        for l in range(levels):
            store = pltpu.make_async_copy(
                out_ref.at[s, pl.ds(l * EDGE, EDGE)], out_hbm.at[l, pl.ds(starts[s], EDGE)], out_sem.at[s, l]
            )
            store.start()
            stores.append(store)
    for store in stores:
        store.wait()


def on_device(state_anom, obs_anom, obs_weight, obs_cell, sector_of):
    f32 = jnp.float32
    regions, owners = lax.axis_size("region"), lax.axis_size("state")
    levels, columns, members = state_anom.shape[1:]
    count = obs_anom.shape[1]
    blocks = owners

    assert regions & (regions - 1) == 0
    half_way = regions // 2
    slot = jax.ShapeDtypeStruct((SUB, 2 * (CAP // SUB) * members + LANES), f32)
    pair = jax.ShapeDtypeStruct((SUB, 2 * slot.shape[1] - LANES), f32)
    near = range(1, half_way)
    own_pack, sides, cross, *slots = pl.pallas_call(
        pack_kernel,
        out_shape=[jax.ShapeDtypeStruct((2, SUB, count // SUB * members + LANES), f32)]
        + [jax.ShapeDtypeStruct((half_way + 1, SUB, LANES), jnp.int32), pair]
        + [slot] * len(near),
        in_specs=[HBM] * 4,
        out_specs=[VMEM] * (3 + len(near)),
        scratch_shapes=[
            pltpu.SMEM((regions,), jnp.int32),
            pltpu.VMEM((count, members), f32),
            pltpu.VMEM((count, members), f32),
            pltpu.VMEM((1, count), jnp.int32),
            pltpu.SemaphoreType.DMA((4,)),
        ],
        compiler_params=limit(8),
        name="pack",
    )(*in_hbm(sector_of, obs_anom, obs_weight, obs_cell))
    crossed = exchange(cross, "region", half_way)
    direct = [exchange(slots[k - 1], "region", k) for k in near]
    relayed = pl.pallas_call(
        relay_kernel,
        out_shape=[slot] * len(near),
        in_specs=[VMEM] * 2,
        out_specs=[VMEM] * len(near),
        compiler_params=limit(4),
        name="relay",
    )(sides, crossed)
    passed = [exchange(relayed[k - 1], "region", k) for k in near]
    packs = gather(own_pack, "state")
    halo = pl.pallas_call(
        pick_kernel,
        out_shape=pair,
        in_specs=[VMEM] * (2 + 2 * len(near)),
        out_specs=VMEM,
        compiler_params=limit(4),
        name="pick",
    )(sides, crossed, *direct, *passed)
    halos = [halo] + [exchange(halo, "state", k) for k in range(1, owners)]

    obs = blocks * count
    state = state_anom[0]
    bf16 = jnp.bfloat16
    middle = columns - 2 * EDGE
    edges = (2, levels * EDGE, members)
    halves = (levels * columns, members)
    s_hi, s_lo = pl.pallas_call(
        prep_kernel,
        out_shape=[jax.ShapeDtypeStruct(halves, bf16)] * 2,
        in_specs=[HBM],
        out_specs=[VMEM] * 2,
        scratch_shapes=[pltpu.VMEM(state.shape, f32), pltpu.SemaphoreType.DMA((levels,))],
        compiler_params=limit(8),
        name="prep",
    )(*in_hbm(state))
    flat, tree = jax.tree.flatten(packs)
    total, edge = pl.pallas_call(
        functools.partial(own_kernel, tree),
        out_shape=[jax.ShapeDtypeStruct(state.shape, f32), jax.ShapeDtypeStruct(edges, f32)],
        in_specs=[VMEM] * (2 + len(flat)),
        out_specs=[HBM, VMEM],
        scratch_shapes=[pltpu.VMEM((levels, middle, members), f32)]
        + [pltpu.VMEM((obs, members), bf16)] * 4
        + [pltpu.SemaphoreType.DMA((levels,))],
        cost_estimate=pl.CostEstimate(
            flops=12 * levels * columns * obs * members, bytes_accessed=8 * state.size + 8 * obs * members, transcendentals=0
        ),
        compiler_params=limit(24),
        name="own",
    )(s_hi, s_lo, *flat)
    out = pl.pallas_call(
        functools.partial(halo_kernel, blocks),
        out_shape=jax.ShapeDtypeStruct(state.shape, f32),
        in_specs=[HBM] + [VMEM] * (3 + blocks),
        out_specs=HBM,
        scratch_shapes=[pltpu.VMEM(edges, f32), pltpu.SemaphoreType.DMA((2, levels))],
        input_output_aliases={0: 0},
        compiler_params=limit(16),
        name="halo",
    )(total, edge, s_hi, s_lo, *halos)
    return out[None]


def solution(mesh):
    in_specs = (
        P("region", "state", None, None),
        P("region", "state", None),
        P("region", "state", None),
        P("region", "state"),
        P(),
    )
    out_specs = P("region", "state", None, None)
    return jax.shard_map(on_device, mesh=mesh, in_specs=in_specs, out_specs=out_specs, check_vma=False)
```

```python
import functools

import jax
import jax.numpy as jnp
from jax import lax
from jax.experimental import pallas as pl
from jax.experimental.pallas import tpu as pltpu
from jax.sharding import PartitionSpec as P


SECT_W = 32
LAT = 8
HALF = 4
CAP = 16
EDGE = 2 * HALF * LAT
SUB = 8
LANES = 128
VMEM = pl.BlockSpec(memory_space=pltpu.VMEM)
SMEM = pl.BlockSpec(memory_space=pltpu.SMEM)
HBM = pl.BlockSpec(memory_space=pltpu.HBM)


def limit(mib):
    return pltpu.CompilerParams(vmem_limit_bytes=mib << 20)


def in_hbm(*values):
    return [pltpu.with_memory_space_constraint(value, pltpu.HBM) for value in values]


def target(index, step, size):
    return index ^ step if size & (size - 1) == 0 else (index + step) % size


def exchange(value, axis, step, ring=False):
    size = lax.axis_size(axis)
    pairs = [(i, target(i, step, size)) for i in range(size)]
    if ring and size == 4 and step < 3:
        around = (0, 1, 3, 2)
        by = 1 if step == 1 else 3
        pairs = [(around[i], around[(i + by) % 4]) for i in range(4)]
    return lax.ppermute(value, axis, pairs)


def gather(value, axis):
    size = lax.axis_size(axis)
    steps = (2, 1) if size == 4 else range(size - 1, 0, -1)
    got = {step: exchange(value, axis, step, ring=True) for step in steps}
    if size == 4:
        got[3] = [exchange(got[k][k - 1], axis, k, ring=True) for k in (1, 2)]
    return [(half[0], half[1]) if isinstance(half, list) else half for half in [value] + [got[k] for k in range(1, size)]]


def gaspari(scaled):
    inside = scaled * scaled * (scaled * (scaled * (0.5 - 0.25 * scaled) + 0.625) - 5.0 / 3.0) + 1.0
    floored = jnp.maximum(scaled, 1.0)
    outside = (
        scaled * (scaled * (scaled * (scaled * (scaled / 12.0 - 0.5) + 0.625) + 5.0 / 3.0) - 5.0)
        + 4.0
        - 2.0 / (3.0 * floored)
    )
    return jnp.where(scaled <= 1.0, inside, jnp.where(scaled < 2.0, outside, 0.0))


def taper(first_col, rows, cells, lon_shift):
    cols = first_col + lax.broadcasted_iota(jnp.int32, (rows, cells.shape[1]), 0)
    obs = cells.astype(jnp.int32)
    lon_gap = cols // LAT - (obs // LAT + lon_shift)
    lat_gap = cols % LAT - obs % LAT
    scaled = jnp.sqrt((lon_gap * lon_gap + lat_gap * lat_gap).astype(jnp.float32)) / HALF
    return gaspari(scaled)


def split(value):
    high = value.astype(jnp.bfloat16)
    return high, (value - high.astype(jnp.float32)).astype(jnp.bfloat16)


def product(left, right, dims):
    dot = functools.partial(lax.dot_general, dimension_numbers=(dims, ((), ())), preferred_element_type=jnp.float32)
    return dot(left[0], right[0]) + (dot(left[0], right[1]) + dot(left[1], right[0]))


NT = ((1,), (1,))
NN = ((1,), (0,))


def folded(rows):
    return jnp.concatenate([rows[i : i + SUB] for i in range(0, rows.shape[0], SUB)], axis=1)


def unfolded(tiles, members):
    return jnp.concatenate([tiles[:, i : i + members] for i in range(0, tiles.shape[1], members)], axis=0)


def pack_kernel(sector_hbm, anom_hbm, weight_hbm, cell_hbm, own_ref, *refs):
    side_ref, cross_ref, *near_refs, sector_ref, anom_ref, weight_ref, cell_ref, sems = refs
    count, members = weight_ref.shape
    loads = [
        pltpu.make_async_copy(cell_hbm, cell_ref, sems.at[0]),
        pltpu.make_async_copy(sector_hbm, sector_ref, sems.at[1]),
        pltpu.make_async_copy(weight_hbm.at[0], weight_ref, sems.at[2]),
        pltpu.make_async_copy(anom_hbm.at[0], anom_ref, sems.at[3]),
    ]
    for load in loads:
        load.start()
    regions = lax.axis_size("region")
    half_way = regions // 2
    me = lax.axis_index("region")
    entry = lax.broadcasted_iota(jnp.int32, (count, LANES), 0)
    lane = lax.broadcasted_iota(jnp.int32, (count, LANES), 1)
    picks = [
        jnp.where(entry == start + lane % width, 1.0, 0.0).astype(jnp.bfloat16)
        for start, width in ((0, count), (0, CAP), (count - CAP, CAP))
    ]
    loads[0].wait()
    cells = jnp.broadcast_to(cell_ref[...].astype(jnp.float32), (SUB, count)).astype(jnp.bfloat16)
    spread = [lax.dot_general(cells, pick, (NN, ((), ())), preferred_element_type=jnp.float32) for pick in picks]
    loads[1].wait()
    mine = sector_ref[me]
    far = me ^ half_way
    is_next = lambda first, second: second == lax.rem(first + 1, regions)
    from_left, from_right, to_right = jnp.int32(0), jnp.int32(0), []
    for step in range(1, regions):
        sector = sector_ref[me ^ step]
        from_left = jnp.where(is_next(sector, mine), step, from_left)
        from_right = jnp.where(is_next(mine, sector), step, from_right)
    codes = [from_left, from_right]
    for step in range(1, half_way):
        sector = sector_ref[me ^ step]
        to_right.append(is_next(mine, sector))
        codes.append(is_next(sector_ref[far], sector).astype(jnp.int32))
    for i, code in enumerate(codes):
        side_ref[i] = jnp.broadcast_to(code, (SUB, LANES))
    for load in loads[2:]:
        load.wait()
    half = count // SUB * members
    own_ref[0, :, :half] = folded(anom_ref[...])
    own_ref[1, :, :half] = folded(weight_ref[...])
    own_ref[0, :, half:] = spread[0]
    own_ref[1, :, half:] = spread[0]
    low = (folded(anom_ref[:CAP, :]), folded(weight_ref[:CAP, :]), spread[1])
    high = (folded(anom_ref[count - CAP :, :]), folded(weight_ref[count - CAP :, :]), spread[2])
    wide = CAP // SUB * members
    upper = lax.broadcasted_iota(jnp.int32, (SUB, LANES), 0) >= SUB // 2
    for i, (start, stop) in enumerate(((0, wide), (wide, 2 * wide), (2 * wide, 2 * wide + LANES))):
        if i < 2:
            cross_ref[:, start:stop] = low[i]
            cross_ref[:, 2 * wide + start : 2 * wide + stop] = high[i]
        for near, up in zip(near_refs, to_right):
            near[:, start:stop] = jnp.where(up, high[i], low[i])
    cross_ref[:, 4 * wide :] = jnp.where(upper, high[2], low[2])


def pair_tile(pair_ref, upper, at, width):
    if at < width - LANES:
        at += upper * (width - LANES)
        return pair_ref[:, at : at + LANES]
    row = upper * (SUB // 2)
    return jnp.broadcast_to(pair_ref[row : row + 1, pair_ref.shape[1] - LANES :], (SUB, LANES))


def relay_kernel(side_ref, cross_ref, *pass_refs):
    width = pass_refs[0].shape[1]
    for step, out in enumerate(pass_refs, start=1):
        up = side_ref[1 + step] == 1
        for at in range(0, width, LANES):
            out[:, at : at + LANES] = jnp.where(up, pair_tile(cross_ref, 1, at, width), pair_tile(cross_ref, 0, at, width))


def pick_kernel(side_ref, cross_ref, *refs):
    *slot_refs, halo_ref = refs
    width = slot_refs[0].shape[1]
    half_way = len(slot_refs) // 2 + 1
    near, passed = slot_refs[: half_way - 1], slot_refs[half_way - 1 :]
    upper = lax.broadcasted_iota(jnp.int32, (SUB, LANES), 0) >= SUB // 2
    for at in range(0, width, LANES):
        values = []
        for side in range(2):
            code = side_ref[side]
            value = pair_tile(cross_ref, 1 - side, at, width)
            for step in range(1, half_way):
                value = jnp.where(code == step, near[step - 1][:, at : at + LANES], value)
                value = jnp.where(code == step + half_way, passed[step - 1][:, at : at + LANES], value)
            values.append(value)
        if at < width - LANES:
            for side, value in enumerate(values):
                start = side * (width - LANES) + at
                halo_ref[:, start : start + LANES] = value
        else:
            halo_ref[:, 2 * at :] = jnp.where(upper, values[1], values[0])


def joined(left, right, dims):
    axis = dims[1][0]
    lefts = jnp.concatenate([left[0], left[0], left[1]], axis=1)
    rights = jnp.concatenate([right[0], right[1], right[0]], axis=axis)
    return lax.dot_general(lefts, rights, (dims, ((), ())), preferred_element_type=jnp.float32)


def prep_kernel(state_hbm, hi_ref, lo_ref, state_ref, sems):
    levels, rows = state_ref.shape[:2]
    loads = [pltpu.make_async_copy(state_hbm.at[l], state_ref.at[l], sems.at[l]) for l in range(levels)]
    for load in loads:
        load.start()
    for l in range(levels):
        loads[l].wait()
        here = pl.ds(l * rows, rows)
        hi_ref[here, :], lo_ref[here, :] = split(state_ref[l])


def own_kernel(tree, s_hi, s_lo, *refs):
    *flat, out_hbm, edge_ref, out_ref, a_hi, a_lo, w_hi, w_lo, out_sem = refs
    packs = [pack if isinstance(pack, tuple) else (pack.at[0], pack.at[1]) for pack in jax.tree.unflatten(tree, flat)]
    blocks = len(packs)
    levels, middle, members = out_ref.shape
    rows = middle + 2 * EDGE
    half = packs[0][0].shape[1] - LANES
    count = half // members * SUB
    lane = lax.broadcasted_iota(jnp.int32, (1, LANES), 1)
    for b in range(blocks):
        here = pl.ds(b * count, count)
        a_hi[here, :], a_lo[here, :] = split(unfolded(packs[b][0][:, :half], members))
    for b in range(blocks):
        here = pl.ds(b * count, count)
        w_hi[here, :], w_lo[here, :] = split(unfolded(packs[b][1][:, :half], members))
    each = LANES // count
    groups = []
    for g in range(0, blocks, each):
        cells = packs[g][0][:1, half:]
        for b in range(1, each):
            cells = jnp.where(lane >= b * count, packs[g + b][0][:1, half:], cells)
        groups.append(taper(0, rows, cells, 0) / (members - 1))
    rho = jnp.concatenate(groups, axis=1)
    stores = []
    for l in range(levels):
        here = pl.ds(l * rows, rows)
        covar = product((s_hi[here, :], s_lo[here, :]), (a_hi[...], a_lo[...]), NT) * rho
        total = product(split(covar), (w_hi[...], w_lo[...]), NN)
        out_ref[l] = total[EDGE : rows - EDGE]
        stores.append(pltpu.make_async_copy(out_ref.at[l], out_hbm.at[l, pl.ds(EDGE, middle)], out_sem.at[l]))
        stores[-1].start()
        for side, part in enumerate((slice(0, EDGE), slice(rows - EDGE, rows))):
            edge_ref[side, pl.ds(l * EDGE, EDGE), :] = total[part]
    for store in stores:
        store.wait()


def halo_kernel(blocks, total_hbm, edge_ref, s_hi, s_lo, *refs):
    halo_refs, (out_hbm, out_ref, out_sem) = refs[:blocks], refs[blocks:]
    levels, columns, members = out_hbm.shape
    wide = CAP // SUB * members
    count = blocks * CAP
    starts = (0, columns - EDGE)
    lane = lax.broadcasted_iota(jnp.int32, (1, LANES), 1)
    per = LANES // CAP
    dot = functools.partial(lax.dot_general, dimension_numbers=(NT, ((), ())), preferred_element_type=jnp.float32)
    covars, weights = [], []
    for s, shift in enumerate((-SECT_W, SECT_W)):
        at = 2 * s * wide
        anom = split(jnp.concatenate([unfolded(h[:, at : at + wide], members) for h in halo_refs], axis=0))
        both = jnp.concatenate(anom, axis=0)
        high, low = (
            jnp.concatenate([ref[l * columns + starts[s] : l * columns + starts[s] + EDGE, :] for l in range(levels)], axis=0)
            for ref in (s_hi, s_lo)
        )
        wide_dot = dot(high, both)
        covar = wide_dot[:, :count] + (wide_dot[:, count:] + dot(low, anom[0]))
        row = s * (SUB // 2)
        tiles = [h[row : row + 1, 4 * wide :] for h in halo_refs]
        groups = []
        for g in range(0, blocks, per):
            cells = tiles[g]
            for b in range(1, min(per, blocks - g)):
                cells = jnp.where(lane >= b * CAP, tiles[g + b], cells)
            groups.append(cells)
        cells = jnp.concatenate(groups, axis=1)[:, :count]
        rho = taper(starts[s], EDGE, cells, shift) / (members - 1)
        covars.append(split((covar.reshape(levels, EDGE, -1) * rho[None]).reshape(levels * EDGE, -1)))
        weights.append(split(jnp.concatenate([unfolded(h[:, at + wide : at + 2 * wide], members) for h in halo_refs], axis=0)))
    stores = []
    for s in range(2):
        out_ref[s] = edge_ref[s] + joined(covars[s], weights[s], NN)
        for l in range(levels):
            store = pltpu.make_async_copy(
                out_ref.at[s, pl.ds(l * EDGE, EDGE)], out_hbm.at[l, pl.ds(starts[s], EDGE)], out_sem.at[s, l]
            )
            store.start()
            stores.append(store)
    for store in stores:
        store.wait()


def on_device(state_anom, obs_anom, obs_weight, obs_cell, sector_of):
    f32 = jnp.float32
    regions, owners = lax.axis_size("region"), lax.axis_size("state")
    levels, columns, members = state_anom.shape[1:]
    count = obs_anom.shape[1]
    blocks = owners

    assert regions & (regions - 1) == 0
    half_way = regions // 2
    slot = jax.ShapeDtypeStruct((SUB, 2 * (CAP // SUB) * members + LANES), f32)
    pair = jax.ShapeDtypeStruct((SUB, 2 * slot.shape[1] - LANES), f32)
    near = range(1, half_way)
    own_pack, sides, cross, *slots = pl.pallas_call(
        pack_kernel,
        out_shape=[jax.ShapeDtypeStruct((2, SUB, count // SUB * members + LANES), f32)]
        + [jax.ShapeDtypeStruct((half_way + 1, SUB, LANES), jnp.int32), pair]
        + [slot] * len(near),
        in_specs=[HBM] * 4,
        out_specs=[VMEM] * (3 + len(near)),
        scratch_shapes=[
            pltpu.SMEM((regions,), jnp.int32),
            pltpu.VMEM((count, members), f32),
            pltpu.VMEM((count, members), f32),
            pltpu.VMEM((1, count), jnp.int32),
            pltpu.SemaphoreType.DMA((4,)),
        ],
        compiler_params=limit(8),
        name="pack",
    )(*in_hbm(sector_of, obs_anom, obs_weight, obs_cell))
    crossed = exchange(cross, "region", half_way)
    direct = [exchange(slots[k - 1], "region", k) for k in near]
    relayed = pl.pallas_call(
        relay_kernel,
        out_shape=[slot] * len(near),
        in_specs=[VMEM] * 2,
        out_specs=[VMEM] * len(near),
        compiler_params=limit(4),
        name="relay",
    )(sides, crossed)
    passed = [exchange(relayed[k - 1], "region", k) for k in near]
    packs = gather(own_pack, "state")
    halo = pl.pallas_call(
        pick_kernel,
        out_shape=pair,
        in_specs=[VMEM] * (2 + 2 * len(near)),
        out_specs=VMEM,
        compiler_params=limit(4),
        name="pick",
    )(sides, crossed, *direct, *passed)
    halos = [halo] + [exchange(halo, "state", k, ring=True) for k in range(1, owners)]

    obs = blocks * count
    state = state_anom[0]
    bf16 = jnp.bfloat16
    middle = columns - 2 * EDGE
    edges = (2, levels * EDGE, members)
    halves = (levels * columns, members)
    s_hi, s_lo = pl.pallas_call(
        prep_kernel,
        out_shape=[jax.ShapeDtypeStruct(halves, bf16)] * 2,
        in_specs=[HBM],
        out_specs=[VMEM] * 2,
        scratch_shapes=[pltpu.VMEM(state.shape, f32), pltpu.SemaphoreType.DMA((levels,))],
        compiler_params=limit(8),
        name="prep",
    )(*in_hbm(state))
    flat, tree = jax.tree.flatten(packs)
    total, edge = pl.pallas_call(
        functools.partial(own_kernel, tree),
        out_shape=[jax.ShapeDtypeStruct(state.shape, f32), jax.ShapeDtypeStruct(edges, f32)],
        in_specs=[VMEM] * (2 + len(flat)),
        out_specs=[HBM, VMEM],
        scratch_shapes=[pltpu.VMEM((levels, middle, members), f32)]
        + [pltpu.VMEM((obs, members), bf16)] * 4
        + [pltpu.SemaphoreType.DMA((levels,))],
        cost_estimate=pl.CostEstimate(
            flops=12 * levels * columns * obs * members, bytes_accessed=8 * state.size + 8 * obs * members, transcendentals=0
        ),
        compiler_params=limit(24),
        name="own",
    )(s_hi, s_lo, *flat)
    out = pl.pallas_call(
        functools.partial(halo_kernel, blocks),
        out_shape=jax.ShapeDtypeStruct(state.shape, f32),
        in_specs=[HBM] + [VMEM] * (3 + blocks),
        out_specs=HBM,
        scratch_shapes=[pltpu.VMEM(edges, f32), pltpu.SemaphoreType.DMA((2, levels))],
        input_output_aliases={0: 0},
        compiler_params=limit(16),
        name="halo",
    )(total, edge, s_hi, s_lo, *halos)
    return out[None]


def solution(mesh):
    in_specs = (
        P("region", "state", None, None),
        P("region", "state", None),
        P("region", "state", None),
        P("region", "state"),
        P(),
    )
    out_specs = P("region", "state", None, None)
    return jax.shard_map(on_device, mesh=mesh, in_specs=in_specs, out_specs=out_specs, check_vma=False)
```

```python
import functools

import jax
import jax.numpy as jnp
from jax import lax
from jax.experimental import pallas as pl
from jax.experimental.pallas import tpu as pltpu
from jax.sharding import PartitionSpec as P


SECT_W = 32
LAT = 8
HALF = 4
CAP = 16
EDGE = 2 * HALF * LAT
SUB = 8
LANES = 128
VMEM = pl.BlockSpec(memory_space=pltpu.VMEM)
SMEM = pl.BlockSpec(memory_space=pltpu.SMEM)
HBM = pl.BlockSpec(memory_space=pltpu.HBM)


def limit(mib):
    return pltpu.CompilerParams(vmem_limit_bytes=mib << 20)


def in_hbm(*values):
    return [pltpu.with_memory_space_constraint(value, pltpu.HBM) for value in values]


def target(index, step, size):
    return index ^ step if size & (size - 1) == 0 else (index + step) % size


def exchange(value, axis, step, ring=False):
    size = lax.axis_size(axis)
    pairs = [(i, target(i, step, size)) for i in range(size)]
    if ring and size == 4 and step < 3:
        around = (0, 1, 3, 2)
        by = 1 if step == 1 else 3
        pairs = [(around[i], around[(i + by) % 4]) for i in range(4)]
    return lax.ppermute(value, axis, pairs)


def gather(value, axis):
    size = lax.axis_size(axis)
    steps = (2, 1) if size == 4 else range(size - 1, 0, -1)
    got = {step: exchange(value, axis, step, ring=True) for step in steps}
    if size == 4:
        got[3] = [exchange(got[k][k - 1], axis, k, ring=True) for k in (1, 2)]
    return [(half[0], half[1]) if isinstance(half, list) else half for half in [value] + [got[k] for k in range(1, size)]]


def gaspari(scaled):
    inside = scaled * scaled * (scaled * (scaled * (0.5 - 0.25 * scaled) + 0.625) - 5.0 / 3.0) + 1.0
    floored = jnp.maximum(scaled, 1.0)
    outside = (
        scaled * (scaled * (scaled * (scaled * (scaled / 12.0 - 0.5) + 0.625) + 5.0 / 3.0) - 5.0)
        + 4.0
        - 2.0 / (3.0 * floored)
    )
    return jnp.where(scaled <= 1.0, inside, jnp.where(scaled < 2.0, outside, 0.0))


def taper(first_col, rows, cells, lon_shift):
    cols = first_col + lax.broadcasted_iota(jnp.int32, (rows, cells.shape[1]), 0)
    obs = cells.astype(jnp.int32)
    lon_gap = cols // LAT - (obs // LAT + lon_shift)
    lat_gap = cols % LAT - obs % LAT
    scaled = jnp.sqrt((lon_gap * lon_gap + lat_gap * lat_gap).astype(jnp.float32)) / HALF
    return gaspari(scaled)


def split(value):
    high = value.astype(jnp.bfloat16)
    return high, (value - high.astype(jnp.float32)).astype(jnp.bfloat16)


def product(left, right, dims):
    dot = functools.partial(lax.dot_general, dimension_numbers=(dims, ((), ())), preferred_element_type=jnp.float32)
    return dot(left[0], right[0]) + (dot(left[0], right[1]) + dot(left[1], right[0]))


NT = ((1,), (1,))
NN = ((1,), (0,))


def folded(rows):
    return jnp.concatenate([rows[i : i + SUB] for i in range(0, rows.shape[0], SUB)], axis=1)


def unfolded(tiles, members):
    return jnp.concatenate([tiles[:, i : i + members] for i in range(0, tiles.shape[1], members)], axis=0)


def pack_kernel(sector_hbm, anom_hbm, weight_hbm, cell_hbm, own_ref, *refs):
    side_ref, cross_ref, *near_refs, sector_ref, anom_ref, weight_ref, cell_ref, sems = refs
    count, members = weight_ref.shape
    loads = [
        pltpu.make_async_copy(cell_hbm, cell_ref, sems.at[0]),
        pltpu.make_async_copy(sector_hbm, sector_ref, sems.at[1]),
        pltpu.make_async_copy(weight_hbm.at[0], weight_ref, sems.at[2]),
        pltpu.make_async_copy(anom_hbm.at[0], anom_ref, sems.at[3]),
    ]
    for load in loads:
        load.start()
    regions = lax.axis_size("region")
    half_way = regions // 2
    me = lax.axis_index("region")
    entry = lax.broadcasted_iota(jnp.int32, (count, LANES), 0)
    lane = lax.broadcasted_iota(jnp.int32, (count, LANES), 1)
    picks = [
        jnp.where(entry == start + lane % width, 1.0, 0.0).astype(jnp.bfloat16)
        for start, width in ((0, count), (0, CAP), (count - CAP, CAP))
    ]
    loads[0].wait()
    cells = jnp.broadcast_to(cell_ref[...].astype(jnp.float32), (SUB, count)).astype(jnp.bfloat16)
    spread = [lax.dot_general(cells, pick, (NN, ((), ())), preferred_element_type=jnp.float32) for pick in picks]
    loads[1].wait()
    mine = sector_ref[me]
    far = me ^ half_way
    is_next = lambda first, second: second == lax.rem(first + 1, regions)
    from_left, from_right, to_right = jnp.int32(0), jnp.int32(0), []
    for step in range(1, regions):
        sector = sector_ref[me ^ step]
        from_left = jnp.where(is_next(sector, mine), step, from_left)
        from_right = jnp.where(is_next(mine, sector), step, from_right)
    codes = [from_left, from_right]
    for step in range(1, half_way):
        sector = sector_ref[me ^ step]
        to_right.append(is_next(mine, sector))
        codes.append(is_next(sector_ref[far], sector).astype(jnp.int32))
    for i, code in enumerate(codes):
        side_ref[i] = jnp.broadcast_to(code, (SUB, LANES))
    for load in loads[2:]:
        load.wait()
    half = count // SUB * members
    own_ref[0, :, :half] = folded(anom_ref[...])
    own_ref[1, :, :half] = folded(weight_ref[...])
    own_ref[0, :, half:] = spread[0]
    own_ref[1, :, half:] = spread[0]
    low = (folded(anom_ref[:CAP, :]), folded(weight_ref[:CAP, :]), spread[1])
    high = (folded(anom_ref[count - CAP :, :]), folded(weight_ref[count - CAP :, :]), spread[2])
    wide = CAP // SUB * members
    upper = lax.broadcasted_iota(jnp.int32, (SUB, LANES), 0) >= SUB // 2
    for i, (start, stop) in enumerate(((0, wide), (wide, 2 * wide), (2 * wide, 2 * wide + LANES))):
        if i < 2:
            cross_ref[:, start:stop] = low[i]
            cross_ref[:, 2 * wide + start : 2 * wide + stop] = high[i]
        for near, up in zip(near_refs, to_right):
            near[:, start:stop] = jnp.where(up, high[i], low[i])
    cross_ref[:, 4 * wide :] = jnp.where(upper, high[2], low[2])


def pair_tile(pair_ref, upper, at, width):
    if at < width - LANES:
        at += upper * (width - LANES)
        return pair_ref[:, at : at + LANES]
    row = upper * (SUB // 2)
    return jnp.broadcast_to(pair_ref[row : row + 1, pair_ref.shape[1] - LANES :], (SUB, LANES))


def relay_kernel(side_ref, cross_ref, *pass_refs):
    width = pass_refs[0].shape[1]
    for step, out in enumerate(pass_refs, start=1):
        up = side_ref[1 + step] == 1
        for at in range(0, width, LANES):
            out[:, at : at + LANES] = jnp.where(up, pair_tile(cross_ref, 1, at, width), pair_tile(cross_ref, 0, at, width))


def pick_kernel(side_ref, cross_ref, *refs):
    *slot_refs, halo_ref = refs
    width = slot_refs[0].shape[1]
    half_way = len(slot_refs) // 2 + 1
    near, passed = slot_refs[: half_way - 1], slot_refs[half_way - 1 :]
    upper = lax.broadcasted_iota(jnp.int32, (SUB, LANES), 0) >= SUB // 2
    for at in range(0, width, LANES):
        values = []
        for side in range(2):
            code = side_ref[side]
            value = pair_tile(cross_ref, 1 - side, at, width)
            for step in range(1, half_way):
                value = jnp.where(code == step, near[step - 1][:, at : at + LANES], value)
                value = jnp.where(code == step + half_way, passed[step - 1][:, at : at + LANES], value)
            values.append(value)
        if at < width - LANES:
            for side, value in enumerate(values):
                start = side * (width - LANES) + at
                halo_ref[:, start : start + LANES] = value
        else:
            halo_ref[:, 2 * at :] = jnp.where(upper, values[1], values[0])


def prep_kernel(state_hbm, hi_ref, lo_ref, state_ref, sems):
    levels, rows = state_ref.shape[:2]
    loads = [pltpu.make_async_copy(state_hbm.at[l], state_ref.at[l], sems.at[l]) for l in range(levels)]
    for load in loads:
        load.start()
    for l in range(levels):
        loads[l].wait()
        here = pl.ds(l * rows, rows)
        hi_ref[here, :], lo_ref[here, :] = split(state_ref[l])


def own_kernel(tree, s_hi, s_lo, *refs):
    *flat, out_hbm, edge_ref, out_ref, a_hi, a_lo, w_hi, w_lo, out_sem = refs
    packs = [pack if isinstance(pack, tuple) else (pack.at[0], pack.at[1]) for pack in jax.tree.unflatten(tree, flat)]
    blocks = len(packs)
    levels, middle, members = out_ref.shape
    rows = middle + 2 * EDGE
    half = packs[0][0].shape[1] - LANES
    count = half // members * SUB
    lane = lax.broadcasted_iota(jnp.int32, (1, LANES), 1)
    for b in range(blocks):
        here = pl.ds(b * count, count)
        a_hi[here, :], a_lo[here, :] = split(unfolded(packs[b][0][:, :half], members))
    for b in range(blocks):
        here = pl.ds(b * count, count)
        w_hi[here, :], w_lo[here, :] = split(unfolded(packs[b][1][:, :half], members))
    each = LANES // count
    groups = []
    for g in range(0, blocks, each):
        cells = packs[g][0][:1, half:]
        for b in range(1, each):
            cells = jnp.where(lane >= b * count, packs[g + b][0][:1, half:], cells)
        groups.append(taper(0, rows, cells, 0) / (members - 1))
    rho = jnp.concatenate(groups, axis=1)
    stores = []
    for l in range(levels):
        here = pl.ds(l * rows, rows)
        covar = product((s_hi[here, :], s_lo[here, :]), (a_hi[...], a_lo[...]), NT) * rho
        total = product(split(covar), (w_hi[...], w_lo[...]), NN)
        out_ref[l] = total[EDGE : rows - EDGE]
        stores.append(pltpu.make_async_copy(out_ref.at[l], out_hbm.at[l, pl.ds(EDGE, middle)], out_sem.at[l]))
        stores[-1].start()
        for side, part in enumerate((slice(0, EDGE), slice(rows - EDGE, rows))):
            edge_ref[side, pl.ds(l * EDGE, EDGE), :] = total[part]
    for store in stores:
        store.wait()


def halo_kernel(blocks, total_hbm, edge_ref, s_hi, s_lo, *refs):
    halo_refs, (out_hbm, out_ref, out_sem) = refs[:blocks], refs[blocks:]
    levels, columns, members = out_hbm.shape
    wide = CAP // SUB * members
    count = blocks * CAP
    starts = (0, columns - EDGE)
    lane = lax.broadcasted_iota(jnp.int32, (1, LANES), 1)
    per = LANES // CAP
    dot = functools.partial(lax.dot_general, dimension_numbers=(NT, ((), ())), preferred_element_type=jnp.float32)
    covars, weights = [], []
    for s, shift in enumerate((-SECT_W, SECT_W)):
        at = 2 * s * wide
        anom = split(jnp.concatenate([unfolded(h[:, at : at + wide], members) for h in halo_refs], axis=0))
        both = jnp.concatenate([anom[0], anom[0], anom[1], anom[1]], axis=0)
        high, low = (
            jnp.concatenate([ref[l * columns + starts[s] : l * columns + starts[s] + EDGE, :] for l in range(levels)], axis=0)
            for ref in (s_hi, s_lo)
        )
        wide_dot = dot(high, both)
        covar = wide_dot[:, : 2 * count] + (wide_dot[:, 2 * count :] + dot(low, both[: 2 * count]))
        row = s * (SUB // 2)
        tiles = [h[row : row + 1, 4 * wide :] for h in halo_refs] * 2
        groups = []
        for g in range(0, 2 * blocks, per):
            cells = tiles[g]
            for b in range(1, min(per, 2 * blocks - g)):
                cells = jnp.where(lane >= b * CAP, tiles[g + b], cells)
            groups.append(cells)
        cells = jnp.concatenate(groups, axis=1)[:, : 2 * count]
        rho = taper(starts[s], EDGE, cells, shift) / (members - 1)
        covars.append(split((covar.reshape(levels, EDGE, -1) * rho[None]).reshape(levels * EDGE, -1)))
        weights.append(split(jnp.concatenate([unfolded(h[:, at + wide : at + 2 * wide], members) for h in halo_refs], axis=0)))
    stores = []
    for s in range(2):
        lefts = jnp.concatenate(covars[s], axis=1)
        rights = jnp.concatenate(weights[s] * 2, axis=0)
        out_ref[s] = edge_ref[s] + lax.dot_general(lefts, rights, (NN, ((), ())), preferred_element_type=jnp.float32)
        for l in range(levels):
            store = pltpu.make_async_copy(
                out_ref.at[s, pl.ds(l * EDGE, EDGE)], out_hbm.at[l, pl.ds(starts[s], EDGE)], out_sem.at[s, l]
            )
            store.start()
            stores.append(store)
    for store in stores:
        store.wait()


def on_device(state_anom, obs_anom, obs_weight, obs_cell, sector_of):
    f32 = jnp.float32
    regions, owners = lax.axis_size("region"), lax.axis_size("state")
    levels, columns, members = state_anom.shape[1:]
    count = obs_anom.shape[1]
    blocks = owners

    assert regions & (regions - 1) == 0
    half_way = regions // 2
    slot = jax.ShapeDtypeStruct((SUB, 2 * (CAP // SUB) * members + LANES), f32)
    pair = jax.ShapeDtypeStruct((SUB, 2 * slot.shape[1] - LANES), f32)
    near = range(1, half_way)
    own_pack, sides, cross, *slots = pl.pallas_call(
        pack_kernel,
        out_shape=[jax.ShapeDtypeStruct((2, SUB, count // SUB * members + LANES), f32)]
        + [jax.ShapeDtypeStruct((half_way + 1, SUB, LANES), jnp.int32), pair]
        + [slot] * len(near),
        in_specs=[HBM] * 4,
        out_specs=[VMEM] * (3 + len(near)),
        scratch_shapes=[
            pltpu.SMEM((regions,), jnp.int32),
            pltpu.VMEM((count, members), f32),
            pltpu.VMEM((count, members), f32),
            pltpu.VMEM((1, count), jnp.int32),
            pltpu.SemaphoreType.DMA((4,)),
        ],
        compiler_params=limit(8),
        name="pack",
    )(*in_hbm(sector_of, obs_anom, obs_weight, obs_cell))
    crossed = exchange(cross, "region", half_way)
    direct = [exchange(slots[k - 1], "region", k) for k in near]
    relayed = pl.pallas_call(
        relay_kernel,
        out_shape=[slot] * len(near),
        in_specs=[VMEM] * 2,
        out_specs=[VMEM] * len(near),
        compiler_params=limit(4),
        name="relay",
    )(sides, crossed)
    passed = [exchange(relayed[k - 1], "region", k) for k in near]
    packs = gather(own_pack, "state")
    halo = pl.pallas_call(
        pick_kernel,
        out_shape=pair,
        in_specs=[VMEM] * (2 + 2 * len(near)),
        out_specs=VMEM,
        compiler_params=limit(4),
        name="pick",
    )(sides, crossed, *direct, *passed)
    halos = [halo] + [exchange(halo, "state", k, ring=True) for k in range(1, owners)]

    obs = blocks * count
    state = state_anom[0]
    bf16 = jnp.bfloat16
    middle = columns - 2 * EDGE
    edges = (2, levels * EDGE, members)
    halves = (levels * columns, members)
    s_hi, s_lo = pl.pallas_call(
        prep_kernel,
        out_shape=[jax.ShapeDtypeStruct(halves, bf16)] * 2,
        in_specs=[HBM],
        out_specs=[VMEM] * 2,
        scratch_shapes=[pltpu.VMEM(state.shape, f32), pltpu.SemaphoreType.DMA((levels,))],
        compiler_params=limit(8),
        name="prep",
    )(*in_hbm(state))
    flat, tree = jax.tree.flatten(packs)
    total, edge = pl.pallas_call(
        functools.partial(own_kernel, tree),
        out_shape=[jax.ShapeDtypeStruct(state.shape, f32), jax.ShapeDtypeStruct(edges, f32)],
        in_specs=[VMEM] * (2 + len(flat)),
        out_specs=[HBM, VMEM],
        scratch_shapes=[pltpu.VMEM((levels, middle, members), f32)]
        + [pltpu.VMEM((obs, members), bf16)] * 4
        + [pltpu.SemaphoreType.DMA((levels,))],
        cost_estimate=pl.CostEstimate(
            flops=12 * levels * columns * obs * members, bytes_accessed=8 * state.size + 8 * obs * members, transcendentals=0
        ),
        compiler_params=limit(24),
        name="own",
    )(s_hi, s_lo, *flat)
    out = pl.pallas_call(
        functools.partial(halo_kernel, blocks),
        out_shape=jax.ShapeDtypeStruct(state.shape, f32),
        in_specs=[HBM] + [VMEM] * (3 + blocks),
        out_specs=HBM,
        scratch_shapes=[pltpu.VMEM(edges, f32), pltpu.SemaphoreType.DMA((2, levels))],
        input_output_aliases={0: 0},
        compiler_params=limit(16),
        name="halo",
    )(total, edge, s_hi, s_lo, *halos)
    return out[None]


def solution(mesh):
    in_specs = (
        P("region", "state", None, None),
        P("region", "state", None),
        P("region", "state", None),
        P("region", "state"),
        P(),
    )
    out_specs = P("region", "state", None, None)
    return jax.shard_map(on_device, mesh=mesh, in_specs=in_specs, out_specs=out_specs, check_vma=False)
```
